32 devices in a mesh: dp: 8 (over y, x, core), seq: 4 (over z).
Axes of the slice: x: 2, y: 2, z: 4, core: 2. Of those that a mesh axis runs over, the one named last changes fastest.
Arguments:
- token_rows: bfloat16 [40960, 5120], P(('dp', 'seq')), may hold values from -6 to 6
- key_rows: bfloat16 [40960, 128], P(('dp', 'seq')), may hold values from -1.8 to 1.8
- query_rows: bfloat16 [40960, 128], P(('dp', 'seq')), may hold values from -0.1796875 to 0.1796875
- step_rows: bfloat16 [40960, 80], P(('dp', 'seq')), may hold values from -6 to 1000
- decay_log: float32 [80], replicated, may hold values from -9.3 to -1.8
- skip_gain: float32 [80], replicated, may hold values from 0.5 to 1.5
- source_rows: int32 [8, 5120], P('dp', 'seq'), may hold values from 0 to 40959, as said below
- document_starts: int32 [8, 6], P('dp'), may hold values from 0 to 5119, as said below
Outputs:
- layer_result_rows: bfloat16 [8, 5120, 5120], P('dp', 'seq')
The draws below stay inside these ranges and needn't reach their ends.
Inputs may be any that keep to these rules, and one draw needn't show every extreme that they name: `source_rows`: every loaded row is placed exactly once. The row at position p of a packed sequence is held by a device whose seq index is p // 1280. Positions come in aligned runs of 8 that hold consecutive rows of one device. A device takes at most 168 of its positions from any one device, and in every seq index some pair of devices reaches that number. `document_starts`: each row is strictly increasing and begins with 0.
All inputs are finite; a program needn't handle non-finite values.
Results may differ from the reference program's by a relative error of at most 0.0065.
Values may be sent and summed in bfloat16 or wider, within the bound.
A program may use at most 192 MiB of HBM per device.

```python
import math
import jax
import jax.numpy as jnp
from jax import lax

HEADS = 80
HEAD_DIM = 64
STATE = 128
SPAN = 256
SEG = 8
NDOC = 6
TOK_DEV = 1280
BINS = 8
LEN = 5120
ROWS = 40960
CAP = 168
WIDTH = 5120


def sudden_rows(key):
    hits = jax.random.randint(jax.random.fold_in(key, 11), (ROWS, 1), 0, max(LEN // 2, 2))
    return hits == 0


def draw_step_rows(key, part):
    offset_key = jax.random.fold_in(key, 21)
    rough_key = jax.random.fold_in(key, 22)
    start_offsets = jax.random.uniform(offset_key, (ROWS // TOK_DEV, 1), jnp.float32, -1.0, 1.0)
    start_offsets = jnp.repeat(start_offsets, TOK_DEV, axis=0)
    jitter_level = jnp.clip(jax.random.normal(rough_key, (ROWS, HEADS), jnp.float32), -4.0, 4.0)
    unscaled_steps = jnp.where(sudden_rows(key), 1000.0, -1.0 + start_offsets + jitter_level)
    return unscaled_steps.astype(jnp.bfloat16)


def draw_key_rows(key, part):
    base_key = jax.random.fold_in(key, 23)
    table_items = jnp.clip(0.3 * jax.random.normal(base_key, (ROWS, STATE), jnp.float32), -1.8, 1.8)
    table_items = jnp.where(sudden_rows(key), 0.002 * table_items, table_items)
    return table_items.astype(jnp.bfloat16)


def draw_decay_log(key, part):
    ranking = jax.random.permutation(jax.random.fold_in(key, 31), HEADS)
    slow_count = HEADS // 2
    slow_heads = ranking < slow_count
    spread = jax.random.uniform(jax.random.fold_in(key, 32), (HEADS,), jnp.float32, 0.0, 1.0)
    slow_log = math.log(0.0001) + spread * math.log(4.0)
    fast_log = math.log(0.05) + spread * math.log(3.0)
    return jnp.where(slow_heads, slow_log, fast_log).astype(jnp.float32)


def shuffle_segments(subkey):
    return jax.random.permutation(subkey, TOK_DEV // SEG)


def draw_source_rows(key, part):
    shard_number = LEN // TOK_DEV
    segment_count = TOK_DEV // SEG
    most_segments = CAP // SEG
    columns = []
    for column in range(shard_number):
        column_key = jax.random.fold_in(key, 100 + column)
        subkeys = jax.random.split(column_key, 6)
        heavy = jax.random.randint(subkeys[0], (), 0, BINS)
        offset_start = jax.random.randint(subkeys[1], (), 0, BINS - 1)
        others = (heavy + 1 + (offset_start + jnp.arange(segment_count - most_segments)) % (BINS - 1)) % BINS
        shifts = jnp.concatenate([jnp.full((most_segments,), heavy), others])
        first_perm = jax.random.permutation(subkeys[2], BINS)
        second_perm = jax.random.permutation(subkeys[3], BINS)
        sources = first_perm[(second_perm[:, None] + shifts[None, :]) % BINS]
        source_order = jax.vmap(shuffle_segments)(jax.random.split(subkeys[4], BINS))
        slot_order = jax.vmap(shuffle_segments)(jax.random.split(subkeys[5], BINS))
        source_at = jnp.take_along_axis(sources, slot_order, axis=1)
        segment_at = source_order[source_at, slot_order]
        inside = jnp.arange(SEG)
        row_start = (source_at * shard_number + column) * TOK_DEV + segment_at * SEG
        placed = row_start[:, :, None] + inside[None, None, :]
        columns.append(placed.reshape(BINS, TOK_DEV))
    return jnp.concatenate(columns, axis=1).astype(jnp.int32)


def pick_starts(subkey):
    chosen = jax.random.permutation(subkey, LEN - 1)[:NDOC - 1] + 1
    return jnp.sort(jnp.concatenate([jnp.zeros((1,), jnp.int32), chosen.astype(jnp.int32)]))


def draw_document_starts(key, part):
    return jax.vmap(pick_starts)(jax.random.split(jax.random.fold_in(key, 41), BINS))


def shard_levels(own_key, dims, cuts, least, high):
    level, own = 1.0, jax.random.fold_in(own_key, 6)
    for dim, shards_of in cuts:
        heights = jnp.exp(jax.random.uniform(jax.random.fold_in(own, dim), (shards_of,), jnp.float32, least / len(cuts), high / len(cuts)))
        level = level * jnp.repeat(heights, dims[dim] // shards_of).reshape([-1 if axis == dim else 1 for axis in range(len(dims))])
    return level


def scatter_about(own_key, extent, scale, reach, cuts=(), held_as=jnp.bfloat16):
    values = scale * jax.random.normal(own_key, extent, jnp.float32)
    if cuts:
        values = values * shard_levels(own_key, extent, cuts, -0.22, 0.18)
    return jnp.clip(values, -reach, reach).astype(held_as)


def setup_inputs(seed: int = 0) -> dict:
    splits = jax.random.split(jax.random.key(seed), 9)
    token_rows = scatter_about(splits[0], (ROWS, WIDTH), 1.0, 6.0, ((0, 32),))
    key_rows = draw_key_rows(jax.random.fold_in(splits[8], 71), 0)
    query_rows = scatter_about(splits[2], (ROWS, STATE), 0.03, 0.1796875, ((0, 32),))
    step_rows = draw_step_rows(jax.random.fold_in(splits[8], 71), 0)
    decay_log = draw_decay_log(jax.random.fold_in(splits[8], 71), 0)
    skip_gain = jnp.clip(jax.random.uniform(splits[5], (HEADS,), jnp.float32, 0.5, 1.5), 0.5, 1.5)
    source_rows = draw_source_rows(jax.random.fold_in(splits[8], 71), 0)
    document_starts = draw_document_starts(jax.random.fold_in(splits[8], 71), 0)
    return dict(token_rows=token_rows, key_rows=key_rows, query_rows=query_rows, step_rows=step_rows, decay_log=decay_log, skip_gain=skip_gain, source_rows=source_rows, document_starts=document_starts)


def span_pass(carried, pieces, decay_rate, skip_gain):
    values, keys_span, query_span, unscaled_steps, restart = pieces
    step_sizes = jax.nn.softplus(unscaled_steps.astype(jnp.float32))
    log_decay = -step_sizes * decay_rate[None, :]
    running_total = jnp.cumsum(log_decay, axis=0)
    document = jnp.cumsum(restart.astype(jnp.int32))
    position = jnp.arange(values.shape[0])
    linked = (document[:, None] == document[None, :]) & (position[None, :] <= position[:, None])
    scores = jnp.dot(query_span, keys_span.T, preferred_element_type=jnp.float32)
    decay_gap = running_total.T[:, :, None] - running_total.T[:, None, :]
    masked_gap = jnp.where(linked[None], decay_gap, -jnp.inf)
    weights = (scores[None] * jnp.exp(masked_gap) * step_sizes.T[:, None, :]).astype(jnp.bfloat16)
    within = jnp.einsum("hts,shp->thp", weights.astype(jnp.float32), values.astype(jnp.float32))
    entry_decay = jnp.where((document == 0)[:, None], jnp.exp(running_total), 0.0)
    from_state = jnp.einsum("tn,hnp->thp", query_span.astype(jnp.float32), carried,
                            precision=lax.Precision.HIGHEST) * entry_decay[:, :, None]
    to_end = running_total[-1][None, :] - running_total
    end_weight = jnp.where((document == document[-1])[:, None], jnp.exp(to_end), 0.0) * step_sizes
    scaled_values = (values.astype(jnp.float32) * end_weight[:, :, None]).astype(jnp.bfloat16)
    added_state = jnp.einsum("sn,shp->hnp", keys_span.astype(jnp.float32), scaled_values.astype(jnp.float32))
    retained = jnp.where(document[-1] == 0, jnp.exp(running_total[-1]), 0.0)
    carried = retained[:, None, None] * carried + added_state
    result = within + from_state + skip_gain[None, :, None] * values.astype(jnp.float32)
    return carried, result.astype(jnp.bfloat16)


def reference(token_rows, key_rows, query_rows, step_rows, decay_log, skip_gain, source_rows, document_starts):
    decay_rate = jnp.exp(decay_log)
    span_count = LEN // SPAN

    def advance(carried, pieces):
        return span_pass(carried, pieces, decay_rate, skip_gain)

    def one_sequence(inputs):
        wanted, starts = inputs
        values = jnp.take(token_rows, wanted, axis=0).reshape(span_count, SPAN, HEADS, HEAD_DIM)
        keys_packed = jnp.take(key_rows, wanted, axis=0).reshape(span_count, SPAN, STATE)
        query_packed = jnp.take(query_rows, wanted, axis=0).reshape(span_count, SPAN, STATE)
        steps_packed = jnp.take(step_rows, wanted, axis=0).reshape(span_count, SPAN, HEADS)
        position = jnp.arange(LEN)
        restart = jnp.any(position[:, None] == starts[None, :], axis=1).reshape(span_count, SPAN)
        zero_state = jnp.zeros((HEADS, STATE, HEAD_DIM), jnp.float32)
        final_state, results = lax.scan(advance, zero_state,
                                        (values, keys_packed, query_packed, steps_packed, restart))
        return results.reshape(LEN, HEADS * HEAD_DIM)

    return lax.map(one_sequence, (source_rows, document_starts))
```

```python
import functools

import jax
import jax.numpy as jnp
from jax import lax
from jax.experimental import pallas as pl
from jax.experimental.pallas import tpu as pltpu
from jax.sharding import PartitionSpec as P

SPAN = 256
SEG = 8
RUNS = SPAN // SEG
HALF = SPAN // 2
LANES = 128

f32, bf16 = jnp.float32, jnp.bfloat16
ANY = pl.BlockSpec(memory_space=pl.ANY)
VMEM_LIMIT = 60 * 1024 * 1024


def params(**more):
    return pltpu.CompilerParams(vmem_limit_bytes=VMEM_LIMIT, **more)


def whole(shape):
    return pl.BlockSpec(shape, lambda *_: (0,) * len(shape))


def spread(hilo, ones):
    return jnp.dot(hilo, ones, preferred_element_type=f32)


def split_float(value):
    high = value.astype(bf16)
    low = (value - high.astype(f32)).astype(bf16)
    return jnp.concatenate([high, low], axis=1)


def plan_kernel(groups, shards, runs, capacity, me_ref, wanted_ref, own_ref, send_ref, pick_ref):
    me = me_ref[0]
    earlier = lax.broadcasted_iota(jnp.int32, (runs, runs), 0) < lax.broadcasted_iota(
        jnp.int32, (runs, runs), 1
    )
    earlier = jnp.where(earlier, 1.0, 0.0).astype(bf16)

    def ranks(hit):
        ones = jnp.where(hit, 1.0, 0.0).astype(bf16)
        return jnp.dot(ones, earlier, preferred_element_type=f32).astype(jnp.int32)

    wanted = wanted_ref[...]
    mine = (wanted // runs) // shards == me
    local = wanted % runs
    rank = ranks(mine)
    lane = lax.broadcasted_iota(jnp.int32, (groups, LANES), 1)
    send = jnp.zeros((groups, LANES), jnp.int32)
    for slot in range(capacity):
        chosen = jnp.sum(jnp.where(mine & (rank == slot), local, 0), axis=1, keepdims=True)
        send = jnp.where(lane == slot, chosen, send)
    send_ref[...] = send
    source = (own_ref[...] // runs) // shards
    group = lax.broadcasted_iota(jnp.int32, (groups, runs), 0)
    hit = jnp.broadcast_to(source, (groups, runs)) == group
    pick_ref[...] = jnp.sum(
        jnp.where(hit, group * capacity + ranks(hit), 0), axis=0, keepdims=True
    )


def make_plan(groups, shards, runs, capacity, me, wanted, own):
    send, pick = pl.pallas_call(
        functools.partial(plan_kernel, groups, shards, runs, capacity),
        grid_spec=pltpu.PrefetchScalarGridSpec(
            num_scalar_prefetch=1,
            grid=(1,),
            in_specs=[whole((groups, runs)), whole((1, runs))],
            out_specs=[whole((groups, LANES)), whole((1, runs))],
        ),
        out_shape=[
            jax.ShapeDtypeStruct((groups, LANES), jnp.int32),
            jax.ShapeDtypeStruct((1, runs), jnp.int32),
        ],
        compiler_params=params(),
        name="plan",
    )(me, wanted, own)
    return send, pick


def fused_kernel(
    axes, sizes, send_ref, pick_ref, starts_ref, tokens_hbm, key_hbm, query_hbm, step_hbm, decay_ref, skip_ref, out_hbm,
    token, small, stage, small_stage, landing, small_landing, current, values_ref, added_ref, final_ref,
    cum_ref, bias_ref, entry_ref, end_ref, keys_ref, query_ref, score_ref, through_ref,
    ones_ref, turned_ref, state_ref, base_ref, staged_out, leaving, entering,
    token_sem, small_sem, own_sem, send_sem, recv_sem, current_sem, hop_send, hop_recv, out_sem,
):
    groups, shards = axes
    capacity, spans, chunks, heads, head_width, starts_count = sizes
    width = heads * head_width
    hops = shards - 1
    me = lax.axis_index("dp")
    place = lax.axis_index("seq")

    def token_copy(chunk):
        column = pl.multiple_of(chunk * width, LANES)
        return pltpu.make_async_copy(
            tokens_hbm.at[:, :, pl.ds(column, width)], token, token_sem
        )

    small_parts = [
        pltpu.make_async_copy(source, small.at[:, :, pl.ds(at * LANES, LANES)], small_sem.at[at])
        for at, source in enumerate((key_hbm, query_hbm, step_hbm))
    ]
    for part in small_parts:
        part.start()
    token_copy(0).start()

    @pl.when(place == 0)
    def _():
        entering[...] = jnp.zeros_like(entering)

    barrier = pltpu.get_barrier_semaphore()

    def greet(**device):
        pl.semaphore_signal(barrier, inc=1, device_id=device, device_id_type=pl.DeviceIdType.MESH)

    @pl.loop(1, groups)
    def _(distance):
        greet(dp=lax.rem(me + distance, groups))

    neighbours = 0
    for distance in {1, shards - 1} if shards > 1 else ():
        greet(seq=lax.rem(place + distance, shards))
        neighbours += 1
    pl.semaphore_wait(barrier, groups - 1 + neighbours)

    def scatter(source, buffer, target, sems):
        own, send, recv = sems

        def gather(group):
            start = group * capacity
            for slot in range(capacity):
                buffer[start + slot] = source[send_ref[group, slot]]
            return pl.ds(start, capacity)

        home = pl.ds(me * capacity, capacity)

        @pl.loop(1, groups)
        def _(distance):
            group = lax.rem(me + distance, groups)
            part = gather(group)
            pltpu.make_async_remote_copy(
                src_ref=buffer.at[part], dst_ref=target.at[home], send_sem=send, recv_sem=recv,
                device_id={"dp": group}, device_id_type=pl.DeviceIdType.MESH,
            ).start()

        part = gather(me)
        pltpu.make_async_copy(buffer.at[part], target.at[home], own).start()

    def wait_bytes(ref, sem):
        pltpu.make_async_copy(ref, ref, sem).wait()

    others = pl.ds(0, (groups - 1) * capacity)
    single = pl.ds(0, capacity)

    def arrived(target, own, recv):
        wait_bytes(target.at[others], recv)
        wait_bytes(target.at[single], own)

    def send_chunk(chunk):
        slot = lax.rem(chunk, stage.shape[0])
        token_copy(chunk).wait()

        @pl.when(chunk >= stage.shape[0])
        def _():
            wait_bytes(stage.at[slot, others], send_sem.at[chunk - stage.shape[0]])

        scatter(
            token, stage.at[slot], landing.at[chunk],
            (own_sem.at[chunk], send_sem.at[chunk], recv_sem.at[chunk]),
        )

        @pl.when(chunk + 1 < chunks)
        def _():
            token_copy(chunk + 1).start()

    for part in small_parts:
        part.wait()
    scatter(
        small, small_stage, small_landing,
        (own_sem.at[chunks], send_sem.at[chunks], recv_sem.at[chunks]),
    )
    for chunk in range(min(2, chunks)):
        send_chunk(chunk)
    arrived(small_landing, own_sem.at[chunks], recv_sem.at[chunks])

    row = lax.broadcasted_iota(jnp.int32, (SPAN, SPAN), 0)
    col = lax.broadcasted_iota(jnp.int32, (SPAN, SPAN), 1)
    row_lanes = lax.broadcasted_iota(jnp.int32, (SPAN, LANES), 0)

    def prepare(span, carry):
        total_before, restarts = carry
        picked = jnp.stack(
            [small_landing[pick_ref[0, span * RUNS + run]].astype(f32) for run in range(RUNS)]
        ).reshape(SPAN, 3 * LANES)
        keys = picked[:, :LANES]
        query = picked[:, LANES : 2 * LANES]
        raw = picked[:, 2 * LANES :]
        steps = jnp.maximum(raw, 0.0) + jnp.log1p(jnp.exp(-jnp.abs(raw)))
        log_decay = -steps * jnp.exp(decay_ref[...])
        lower = jnp.where(col <= row, 1.0, 0.0)
        cum = jnp.dot(lower, log_decay, precision=lax.Precision.HIGHEST, preferred_element_type=f32)
        doc_row = jnp.zeros((SPAN, SPAN), jnp.int32)
        doc_col = jnp.zeros((SPAN, SPAN), jnp.int32)
        doc = jnp.zeros((SPAN, LANES), jnp.int32)
        last = jnp.int32(0)
        for number in range(starts_count):
            start = starts_ref[number] - span * SPAN
            inside = (start >= 0) & (start < SPAN)
            at = jnp.where(inside, start, jnp.int32(1 << 20))
            doc_row += (row >= at).astype(jnp.int32)
            doc_col += (col >= at).astype(jnp.int32)
            doc += (row_lanes >= at).astype(jnp.int32)
            last += inside.astype(jnp.int32)
        linked = (doc_row == doc_col) & (col <= row)
        scores = lax.dot_general(
            query.astype(bf16), keys.astype(bf16), (((1,), (1,)), ((), ())),
            preferred_element_type=f32,
        )
        score_ref[span] = jnp.where(linked, scores, 0.0)
        total = cum[SPAN - 1 :, :]
        entry_ref[span] = split_float(jnp.where(doc == 0, jnp.exp(cum), 0.0))
        end_ref[span] = split_float(jnp.where(doc == last, jnp.exp(total - cum), 0.0) * steps)
        cum_ref[span] = cum
        bias_ref[span] = (jnp.log(steps) - cum).T
        keys_ref[span] = keys.T.astype(bf16)
        query_ref[span] = query.astype(bf16)
        return total_before + total, restarts + last

    total, restarts = lax.fori_loop(
        0, spans, prepare, (jnp.zeros((1, LANES), f32), jnp.int32(0))
    )
    through = jnp.where(restarts == 0, jnp.exp(total), 0.0)
    through_ref[...] = split_float(jnp.broadcast_to(through, (16, LANES)))

    def select_heads(chunk):
        wanted = lax.broadcasted_iota(jnp.int32, (LANES, width), 0) - chunk * heads
        own_head = lax.broadcasted_iota(jnp.int32, (LANES, width), 1) // head_width
        ones = jnp.where(wanted == own_head, 1.0, 0.0).astype(bf16)
        ones_ref[pl.ds(0, LANES), :] = ones
        ones_ref[pl.ds(LANES, LANES), :] = ones

    def span_values(slot, span):
        runs = pl.ds(pl.multiple_of(span * RUNS, RUNS), RUNS)
        return values_ref[slot, runs].astype(f32).reshape(SPAN, width)

    ring = values_ref.shape[0]

    def hop_copy(chunk, hop):
        return pltpu.make_async_remote_copy(
            src_ref=leaving.at[chunk, hop], dst_ref=entering.at[chunk, hop],
            send_sem=hop_send.at[chunk, hop], recv_sem=hop_recv.at[chunk, hop],
            device_id={"seq": jnp.minimum(place + 1, shards - 1)},
            device_id_type=pl.DeviceIdType.MESH,
        )

    def pass_on(chunk, hop, state):
        @pl.when(place < shards - 1)
        def _():
            leaving[chunk, hop] = state.astype(bf16)
            hop_copy(chunk, hop).start()

    def wait_hop(chunk, hop):
        @pl.when(place > 0)
        def _():
            wait_bytes(entering.at[chunk, hop], hop_recv.at[chunk, hop])

    def take_chunk(chunk):
        slot = lax.rem(chunk, ring)
        arrived(landing.at[chunk], own_sem.at[chunk], recv_sem.at[chunk])
        copy = pltpu.make_async_copy(landing.at[chunk], current, current_sem)
        copy.start()
        select_heads(chunk)
        copy.wait()

        @pl.loop(0, spans)
        def _(span):
            for run in range(RUNS):
                values_ref[slot, span * RUNS + run] = current[pick_ref[0, span * RUNS + run]]

        final_ref[slot] = jnp.zeros((LANES, width), f32)

        @pl.loop(0, spans)
        def _(span):
            ones = ones_ref[...]
            scaled = (span_values(slot, span) * spread(end_ref[span], ones)).astype(bf16)
            added = jnp.dot(keys_ref[span], scaled, preferred_element_type=f32)
            added_ref[slot, span] = added
            kept = spread(entry_ref[span, pl.ds(SPAN - 16, 16), :], ones)[15:16, :]
            final_ref[slot] = kept * final_ref[slot] + added

        pass_on(chunk, 0, final_ref[slot])

    def forward(chunk, hop):
        slot = lax.rem(chunk, ring)
        wait_hop(chunk, hop - 1)
        select_heads(chunk)
        kept = spread(through_ref[...], ones_ref[...])[0:1, :]
        pass_on(chunk, hop, kept * entering[chunk, hop - 1].astype(f32) + final_ref[slot])

    per_tile = LANES // head_width
    lane = lax.broadcasted_iota(jnp.int32, (HALF, LANES), 1) // head_width

    def out_copy(chunk):
        slot = lax.rem(chunk, 2)
        column = pl.multiple_of(chunk * width, LANES)
        return pltpu.make_async_copy(
            staged_out.at[slot], out_hbm.at[:, pl.ds(column, width)], out_sem.at[slot]
        )

    def finish(chunk):
        slot = lax.rem(chunk, ring)
        put = lax.rem(chunk, 2)
        wait_hop(chunk, hops - 1)
        select_heads(chunk)
        state_ref[...] = entering[chunk, hops - 1].astype(f32)
        first_head = pl.multiple_of(chunk * heads, heads)

        @pl.when(chunk >= 2)
        def _():
            out_copy(chunk - 2).wait()

        @pl.loop(0, spans)
        def _(span):
            values = span_values(slot, span)
            entry = spread(entry_ref[span], ones_ref[...])
            from_state = jnp.dot(
                query_ref[span], state_ref[...].astype(bf16), preferred_element_type=f32
            )
            base_ref[...] = from_state * entry + skip_ref[chunk] * values
            state_ref[...] = entry[SPAN - 1 :, :] * state_ref[...] + added_ref[slot, span]
            turned_ref[...] = pltpu.roll(cum_ref[span], lax.rem(LANES - first_head, LANES), axis=1)
            bias = bias_ref[span, pl.ds(first_head, heads), :]
            packed = values.astype(bf16)
            for tile in range(heads // per_tile):
                columns = slice(tile * LANES, (tile + 1) * LANES)
                for half in range(2):
                    rows = slice(half * HALF, (half + 1) * HALF)
                    depth = (half + 1) * HALF
                    scores = score_ref[span, rows, :depth]
                    total = None
                    for inner in range(per_tile):
                        head = tile * per_tile + inner
                        gap = turned_ref[rows, head : head + 1] + bias[head : head + 1, :depth]
                        weights = (scores * jnp.exp(jnp.minimum(gap, 60.0))).astype(bf16)
                        part = jnp.dot(
                            weights, packed[:depth, columns], preferred_element_type=f32
                        )
                        total = part if total is None else jnp.where(lane == inner, part, total)
                    target = pl.ds(pl.multiple_of(span * SPAN + half * HALF, HALF), HALF)
                    staged_out[put, target, columns] = (base_ref[rows, columns] + total).astype(bf16)

        out_copy(chunk).start()

    @pl.loop(0, chunks + hops)
    def _(step):
        @pl.when(step + 2 < chunks)
        def _():
            send_chunk(step + 2)

        @pl.when(step < chunks)
        def _():
            take_chunk(step)

        for hop in range(1, hops):

            @pl.when((step >= hop) & (step - hop < chunks))
            def _():
                forward(step - hop, hop)

        @pl.when(step >= hops)
        def _():
            finish(step - hops)

    for chunk in range(max(0, chunks - 2), chunks):
        out_copy(chunk).wait()
    for chunk in range(max(0, chunks - stage.shape[0]), chunks):
        wait_bytes(stage.at[chunk % stage.shape[0], others], send_sem.at[chunk])
    wait_bytes(small_stage.at[others], send_sem.at[chunks])

    @pl.when(place < shards - 1)
    def _():
        @pl.loop(0, chunks)
        def _(chunk):
            for hop in range(hops):
                wait_bytes(leaving.at[chunk, hop], hop_send.at[chunk, hop])


CHUNK_HEADS = 8
STAGES = 3


def fused(send, pick, starts, tokens, keys, query, steps, decay, skip, groups, shards, capacity, heads):
    runs, _, full = tokens.shape
    spans = runs // RUNS
    head_width = full // heads
    chunks = heads // CHUNK_HEADS
    width = CHUNK_HEADS * head_width
    hops = shards - 1
    ring = hops + 1
    slots = groups * capacity
    smem = pl.BlockSpec(memory_space=pltpu.SMEM)
    vmem = pl.BlockSpec(memory_space=pltpu.VMEM)
    dma = pltpu.SemaphoreType.DMA
    small = 3 * LANES
    return pl.pallas_call(
        functools.partial(
            fused_kernel, (groups, shards),
            (capacity, spans, chunks, CHUNK_HEADS, head_width, starts.shape[0]),
        ),
        in_specs=[smem, smem, smem, ANY, ANY, ANY, ANY, vmem, vmem],
        out_specs=ANY,
        out_shape=jax.ShapeDtypeStruct((runs * SEG, full), bf16),
        scratch_shapes=[
            pltpu.VMEM((runs, SEG, width), bf16),
            pltpu.VMEM((runs, SEG, small), bf16),
            pltpu.VMEM((STAGES, slots, SEG, width), bf16),
            pltpu.VMEM((slots, SEG, small), bf16),
            pltpu.VMEM((chunks, slots, SEG, width), bf16),
            pltpu.VMEM((slots, SEG, small), bf16),
            pltpu.VMEM((slots, SEG, width), bf16),
            pltpu.VMEM((ring, runs, SEG, width), bf16),
            pltpu.VMEM((ring, spans, LANES, width), f32),
            pltpu.VMEM((ring, LANES, width), f32),
            pltpu.VMEM((spans, SPAN, LANES), f32),
            pltpu.VMEM((spans, LANES, SPAN), f32),
            pltpu.VMEM((spans, SPAN, 2 * LANES), bf16),
            pltpu.VMEM((spans, SPAN, 2 * LANES), bf16),
            pltpu.VMEM((spans, LANES, SPAN), bf16),
            pltpu.VMEM((spans, SPAN, LANES), bf16),
            pltpu.VMEM((spans, SPAN, SPAN), f32),
            pltpu.VMEM((16, 2 * LANES), bf16),
            pltpu.VMEM((2 * LANES, width), bf16),
            pltpu.VMEM((SPAN, LANES), f32),
            pltpu.VMEM((LANES, width), f32),
            pltpu.VMEM((SPAN, width), f32),
            pltpu.VMEM((2, runs * SEG, width), bf16),
            pltpu.VMEM((chunks, hops, LANES, width), bf16),
            pltpu.VMEM((chunks, hops, LANES, width), bf16),
            dma,
            dma((3,)),
            dma((chunks + 1,)),
            dma((chunks + 1,)),
            dma((chunks + 1,)),
            dma,
            dma((chunks, hops)),
            dma((chunks, hops)),
            dma((2,)),
        ],
        compiler_params=params(collective_id=0, has_side_effects=True),
        cost_estimate=pl.CostEstimate(
            flops=8 * runs * SEG * SPAN * full, transcendentals=runs * SEG * SPAN * heads,
            bytes_accessed=4 * runs * SEG * full,
        ),
        name="fused",
    )(send, pick, starts, tokens, keys, query, steps, decay, skip)


def on_device(
    token_rows, key_rows, query_rows, step_rows, decay_log, skip_gain, source_rows, document_starts
):
    tokens, full = token_rows.shape
    groups = lax.axis_size("dp")
    shards = lax.axis_size("seq")
    heads = decay_log.shape[0]
    runs = tokens // SEG
    capacity = runs // groups + 1
    pad = LANES - heads

    own = source_rows[0].reshape(runs, SEG)[:, 0][None, :] // SEG
    wanted = lax.all_to_all(
        jnp.broadcast_to(own, (groups, runs)), "dp", split_axis=0, concat_axis=0, tiled=True
    )
    me = lax.axis_index("dp").astype(jnp.int32)[None]
    send, pick = make_plan(groups, shards, runs, capacity, me, wanted, own)
    starts = document_starts[0] - lax.axis_index("seq").astype(jnp.int32) * tokens
    skip = jnp.repeat(skip_gain, full // heads).reshape(heads // CHUNK_HEADS, 1, -1)
    result = fused(
        send, pick, starts, token_rows.reshape(runs, SEG, full), key_rows.reshape(runs, SEG, LANES),
        query_rows.reshape(runs, SEG, LANES),
        jnp.pad(step_rows, ((0, 0), (0, pad))).reshape(runs, SEG, LANES),
        jnp.pad(decay_log, (0, pad))[None, :], skip, groups, shards, capacity, heads,
    )
    return result[None]


def solution(mesh):
    in_specs = (
        P(("dp", "seq"), None),
        P(("dp", "seq"), None),
        P(("dp", "seq"), None),
        P(("dp", "seq"), None),
        P(),
        P(),
        P("dp", "seq"),
        P("dp", None),
    )
    out_specs = P("dp", "seq", None)
    return jax.shard_map(
        on_device, mesh=mesh, in_specs=in_specs, out_specs=out_specs, check_vma=False
    )
```

```python
import functools

import jax
import jax.numpy as jnp
from jax import lax
from jax.experimental import pallas as pl
from jax.experimental.pallas import tpu as pltpu
from jax.sharding import PartitionSpec as P

SPAN = 256
SEG = 8
RUNS = SPAN // SEG
HALF = SPAN // 2
LANES = 128

f32, bf16 = jnp.float32, jnp.bfloat16
ANY = pl.BlockSpec(memory_space=pl.ANY)
VMEM_LIMIT = 60 * 1024 * 1024


def params(**more):
    return pltpu.CompilerParams(vmem_limit_bytes=VMEM_LIMIT, **more)


def spread(hilo, ones):
    return jnp.dot(hilo, ones, preferred_element_type=f32)


def split_float(value):
    high = value.astype(bf16)
    low = (value - high.astype(f32)).astype(bf16)
    return jnp.concatenate([high, low], axis=1)


def plan_sends(groups, shards, runs, capacity, me, wanted):
    earlier = lax.broadcasted_iota(jnp.int32, (runs, runs), 0) < lax.broadcasted_iota(
        jnp.int32, (runs, runs), 1
    )
    earlier = jnp.where(earlier, 1.0, 0.0).astype(bf16)

    def ranks(hit):
        ones = jnp.where(hit, 1.0, 0.0).astype(bf16)
        return jnp.dot(ones, earlier, preferred_element_type=f32).astype(jnp.int32)

    mine = (wanted // runs) // shards == me
    local = wanted % runs
    rank = ranks(mine)
    lane = lax.broadcasted_iota(jnp.int32, (groups, LANES), 1)
    send = jnp.zeros((groups, LANES), jnp.int32)
    for slot in range(capacity):
        chosen = jnp.sum(jnp.where(mine & (rank == slot), local, 0), axis=1, keepdims=True)
        send = jnp.where(lane == slot, chosen, send)
    return send, ranks


def plan_picks(groups, shards, runs, capacity, own, ranks):
    source = (own // runs) // shards
    group = lax.broadcasted_iota(jnp.int32, (groups, runs), 0)
    hit = jnp.broadcast_to(source, (groups, runs)) == group
    return jnp.sum(jnp.where(hit, group * capacity + ranks(hit), 0), axis=0, keepdims=True)


def fused_kernel(
    axes, sizes, source_ref, starts_ref, tokens_hbm, key_hbm, query_hbm, step_hbm, decay_log_ref, gain_ref, out_hbm,
    own_runs, wanted_runs, plan_ref, choice_ref, send_ref, pick_ref, head_ref, turned_steps,
    token, small, stage, small_stage, landing, small_landing, current, values_ref, added_ref, final_ref,
    cum_ref, bias_ref, entry_ref, end_ref, keys_ref, query_ref, score_ref, through_ref,
    ones_ref, turned_ref, skip_ref, state_ref, staged_out, leaving, entering,
    plan_sem, id_send, id_recv,
    token_sem, small_sem, own_sem, send_sem, recv_sem, current_sem, hop_send, hop_recv, out_sem,
):
    groups, shards = axes
    capacity, spans, chunks, heads, head_width, starts_count = sizes
    width = heads * head_width
    hops = shards - 1
    runs = spans * RUNS
    all_heads = chunks * heads
    me = lax.axis_index("dp")
    place = lax.axis_index("seq")

    def token_copy(chunk):
        column = pl.multiple_of(chunk * width, LANES)
        return pltpu.make_async_copy(
            tokens_hbm.at[:, :, pl.ds(column, width)], token, token_sem
        )

    small_parts = [
        pltpu.make_async_copy(key_hbm, small.at[:, :, pl.ds(0, LANES)], small_sem.at[0]),
        pltpu.make_async_copy(query_hbm, small.at[:, :, pl.ds(LANES, LANES)], small_sem.at[1]),
        pltpu.make_async_copy(step_hbm, turned_steps, small_sem.at[2]),
    ]
    token_copy(0).start()
    for part in small_parts:
        part.start()

    barrier = pltpu.get_barrier_semaphore()

    def greet(**device):
        pl.semaphore_signal(barrier, inc=1, device_id=device, device_id_type=pl.DeviceIdType.MESH)

    @pl.when(place == 0)
    def _():
        entering[...] = jnp.zeros_like(entering)

    @pl.loop(1, groups)
    def _(distance):
        greet(dp=lax.rem(me + distance, groups))

    neighbours = 0
    for distance in {1, shards - 1} if shards > 1 else ():
        greet(seq=lax.rem(place + distance, shards))
        neighbours += 1

    every = lax.broadcasted_iota(jnp.int32, (runs * SEG, runs), 0) == SEG * lax.broadcasted_iota(
        jnp.int32, (runs * SEG, runs), 1
    )
    every = jnp.where(every, 1.0, 0.0).astype(bf16)
    numbers = source_ref[...] // SEG
    parts = [((numbers >> shift) & 255).astype(f32).astype(bf16) for shift in (0, 8, 16)]
    own = jnp.dot(
        jnp.concatenate([jnp.broadcast_to(part, (8, runs * SEG)) for part in parts], axis=0), every,
        preferred_element_type=f32,
    ).astype(jnp.int32)
    own = own[0:1] + own[8:9] * 256 + own[16:17] * 65536
    own_runs[...] = own
    wanted_runs[me] = own
    pl.semaphore_wait(barrier, groups - 1 + neighbours)

    @pl.loop(1, groups)
    def _(distance):
        group = lax.rem(me + distance, groups)
        pltpu.make_async_remote_copy(
            src_ref=own_runs, dst_ref=wanted_runs.at[me], send_sem=id_send, recv_sem=id_recv,
            device_id={"dp": group}, device_id_type=pl.DeviceIdType.MESH,
        ).start()

    def wait_bytes(ref, sem):
        pltpu.make_async_copy(ref, ref, sem).wait()

    wait_bytes(wanted_runs.at[pl.ds(0, groups - 1)], id_recv)
    wanted = jnp.concatenate([wanted_runs[group] for group in range(groups)], axis=0)
    plan_ref[...], ranks = plan_sends(groups, shards, runs, capacity, me, wanted)
    plan_copy = pltpu.make_async_copy(plan_ref, send_ref, plan_sem.at[0])
    plan_copy.start()
    choice_ref[...] = plan_picks(groups, shards, runs, capacity, own, ranks)
    choice_copy = pltpu.make_async_copy(choice_ref, pick_ref, plan_sem.at[1])
    choice_copy.start()
    plan_copy.wait()

    def scatter(source, buffer, target, sems):
        own_done, send, recv = sems

        def gather(group):
            start = group * capacity
            for slot in range(capacity):
                buffer[start + slot] = source[send_ref[group, slot]]
            return pl.ds(start, capacity)

        home = pl.ds(me * capacity, capacity)

        @pl.loop(1, groups)
        def _(distance):
            group = lax.rem(me + distance, groups)
            part = gather(group)
            pltpu.make_async_remote_copy(
                src_ref=buffer.at[part], dst_ref=target.at[home], send_sem=send, recv_sem=recv,
                device_id={"dp": group}, device_id_type=pl.DeviceIdType.MESH,
            ).start()

        part = gather(me)
        pltpu.make_async_copy(buffer.at[part], target.at[home], own_done).start()

    others = pl.ds(0, (groups - 1) * capacity)
    single = pl.ds(0, capacity)

    def arrived(target, own, recv):
        wait_bytes(target.at[others], recv)
        wait_bytes(target.at[single], own)

    def send_chunk(chunk):
        slot = lax.rem(chunk, stage.shape[0])
        token_copy(chunk).wait()

        @pl.when(chunk >= stage.shape[0])
        def _():
            wait_bytes(stage.at[slot, others], send_sem.at[chunk - stage.shape[0]])

        scatter(
            token, stage.at[slot], landing.at[chunk],
            (own_sem.at[chunk], send_sem.at[chunk], recv_sem.at[chunk]),
        )

        @pl.when(chunk + 1 < chunks)
        def _():
            token_copy(chunk + 1).start()

    send_chunk(0)
    for part in small_parts:
        part.wait()
    steps_across = turned_steps[...].astype(f32)
    steps_across = jnp.concatenate(
        [steps_across, jnp.zeros((LANES - all_heads, runs * SEG), f32)], axis=0
    )
    small[:, :, 2 * LANES :] = steps_across.T.reshape(runs, SEG, LANES).astype(bf16)
    scatter(
        small, small_stage, small_landing,
        (own_sem.at[chunks], send_sem.at[chunks], recv_sem.at[chunks]),
    )
    choice_copy.wait()
    if chunks > 1:
        send_chunk(1)
    head_ref[...] = jnp.zeros_like(head_ref)
    head_ref[0:1, :all_heads] = decay_log_ref[...]
    head_ref[8:9, :all_heads] = gain_ref[...]
    skip_ref[...] = split_float(jnp.broadcast_to(head_ref[8:9, :], (16, LANES)))
    arrived(small_landing, own_sem.at[chunks], recv_sem.at[chunks])

    row = lax.broadcasted_iota(jnp.int32, (SPAN, SPAN), 0)
    col = lax.broadcasted_iota(jnp.int32, (SPAN, SPAN), 1)
    row_lanes = lax.broadcasted_iota(jnp.int32, (SPAN, LANES), 0)

    def prepare(span, carry):
        total_before, restarts = carry
        picked = jnp.stack(
            [small_landing[pick_ref[0, span * RUNS + run]].astype(f32) for run in range(RUNS)]
        ).reshape(SPAN, 3 * LANES)
        keys = picked[:, :LANES]
        query = picked[:, LANES : 2 * LANES]
        raw = picked[:, 2 * LANES :]
        steps = jnp.maximum(raw, 0.0) + jnp.log1p(jnp.exp(-jnp.abs(raw)))
        log_decay = -steps * jnp.exp(head_ref[0:1, :])
        lower = jnp.where(col <= row, 1.0, 0.0)
        cum = jnp.dot(lower, log_decay, precision=lax.Precision.HIGHEST, preferred_element_type=f32)
        doc_row = jnp.zeros((SPAN, SPAN), jnp.int32)
        doc_col = jnp.zeros((SPAN, SPAN), jnp.int32)
        doc = jnp.zeros((SPAN, LANES), jnp.int32)
        last = jnp.int32(0)
        for number in range(starts_count):
            start = starts_ref[0, number] - (place * spans + span) * SPAN
            inside = (start >= 0) & (start < SPAN)
            at = jnp.where(inside, start, jnp.int32(1 << 20))
            doc_row += (row >= at).astype(jnp.int32)
            doc_col += (col >= at).astype(jnp.int32)
            doc += (row_lanes >= at).astype(jnp.int32)
            last += inside.astype(jnp.int32)
        linked = (doc_row == doc_col) & (col <= row)
        scores = lax.dot_general(
            query.astype(bf16), keys.astype(bf16), (((1,), (1,)), ((), ())),
            preferred_element_type=f32,
        )
        score_ref[span] = jnp.where(linked, scores, 0.0)
        total = cum[SPAN - 1 :, :]
        entry_ref[span] = split_float(jnp.where(doc == 0, jnp.exp(cum), 0.0))
        end_ref[span] = split_float(jnp.where(doc == last, jnp.exp(total - cum), 0.0) * steps)
        cum_ref[span] = cum
        bias_ref[span] = (jnp.log(steps) - cum).T
        keys_ref[span] = keys.T.astype(bf16)
        query_ref[span] = query.astype(bf16)
        return total_before + total, restarts + last

    total, restarts = lax.fori_loop(
        0, spans, prepare, (jnp.zeros((1, LANES), f32), jnp.int32(0))
    )
    through = jnp.where(restarts == 0, jnp.exp(total), 0.0)
    through_ref[...] = split_float(jnp.broadcast_to(through, (16, LANES)))

    def select_heads(chunk):
        wanted = lax.broadcasted_iota(jnp.int32, (LANES, width), 0) - chunk * heads
        own_head = lax.broadcasted_iota(jnp.int32, (LANES, width), 1) // head_width
        ones = jnp.where(wanted == own_head, 1.0, 0.0).astype(bf16)
        slot = lax.rem(chunk, 2)
        ones_ref[slot, pl.ds(0, LANES), :] = ones
        ones_ref[slot, pl.ds(LANES, LANES), :] = ones

    def span_values(span):
        part = pl.ds(pl.multiple_of(span * RUNS, RUNS), RUNS)
        return values_ref[part].astype(f32).reshape(SPAN, width)

    def hop_copy(chunk, hop):
        return pltpu.make_async_remote_copy(
            src_ref=leaving.at[hop], dst_ref=entering.at[chunk, hop],
            send_sem=hop_send.at[hop], recv_sem=hop_recv.at[chunk, hop],
            device_id={"seq": jnp.minimum(place + 1, shards - 1)},
            device_id_type=pl.DeviceIdType.MESH,
        )

    def pass_on(chunk, hop, state):
        @pl.when((place < shards - 1) & (chunk > 0))
        def _():
            wait_bytes(leaving.at[hop], hop_send.at[hop])

        @pl.when(place < shards - 1)
        def _():
            leaving[hop] = state.astype(bf16)
            hop_copy(chunk, hop).start()

    def wait_hop(chunk, hop):
        @pl.when(place > 0)
        def _():
            wait_bytes(entering.at[chunk, hop], hop_recv.at[chunk, hop])

    def take_chunk(chunk):
        slot = lax.rem(chunk, 2)
        arrived(landing.at[chunk], own_sem.at[chunk], recv_sem.at[chunk])
        copy = pltpu.make_async_copy(landing.at[chunk], current, current_sem)
        copy.start()
        select_heads(chunk)
        copy.wait()
        final_ref[...] = jnp.zeros_like(final_ref)

        @pl.loop(0, spans)
        def _(span):
            for run in range(RUNS):
                values_ref[span * RUNS + run] = current[pick_ref[0, span * RUNS + run]]
            ones = ones_ref[slot]
            scaled = (span_values(span) * spread(end_ref[span], ones)).astype(bf16)
            added = jnp.dot(keys_ref[span], scaled, preferred_element_type=f32)
            added_ref[slot, span] = added
            kept = spread(entry_ref[span, pl.ds(SPAN - 16, 16), :], ones)[15:16, :]
            final_ref[...] = kept * final_ref[...] + added

        pass_on(chunk, 0, final_ref[...])

    def forward(chunk, hop):
        wait_hop(chunk, hop - 1)
        kept = spread(through_ref[...], ones_ref[lax.rem(chunk, 2)])[0:1, :]
        pass_on(chunk, hop, kept * entering[chunk, hop - 1].astype(f32) + final_ref[...])

    per_tile = LANES // head_width
    lane = lax.broadcasted_iota(jnp.int32, (HALF, LANES), 1) // head_width

    def out_copy(chunk):
        slot = lax.rem(chunk, 2)
        column = pl.multiple_of(chunk * width, LANES)
        return pltpu.make_async_copy(
            staged_out.at[slot], out_hbm.at[:, pl.ds(column, width)], out_sem.at[slot]
        )

    def within(chunk, span):
        put = lax.rem(chunk, 2)
        first_head = pl.multiple_of(chunk * heads, heads)
        values = span_values(span)
        skipped = spread(skip_ref[...], ones_ref[put])[0:1, :] * values
        turned_ref[...] = pltpu.roll(cum_ref[span], lax.rem(LANES - first_head, LANES), axis=1)
        bias = bias_ref[span, pl.ds(first_head, heads), :]
        packed = values.astype(bf16)
        for tile in range(heads // per_tile):
            columns = slice(tile * LANES, (tile + 1) * LANES)
            for half in range(2):
                rows = slice(half * HALF, (half + 1) * HALF)
                depth = (half + 1) * HALF
                scores = score_ref[span, rows, :depth]
                total = None
                for inner in range(per_tile):
                    head = tile * per_tile + inner
                    gap = turned_ref[rows, head : head + 1] + bias[head : head + 1, :depth]
                    weights = (scores * jnp.exp(jnp.minimum(gap, 60.0))).astype(bf16)
                    part = jnp.dot(weights, packed[:depth, columns], preferred_element_type=f32)
                    total = part if total is None else jnp.where(lane == inner, part, total)
                target = pl.ds(pl.multiple_of(span * SPAN + half * HALF, HALF), HALF)
                staged_out[put, target, columns] = (skipped[rows, columns] + total).astype(bf16)

    def complete(chunk):
        slot = lax.rem(chunk, 2)
        wait_hop(chunk, hops - 1)
        state_ref[...] = entering[chunk, hops - 1].astype(f32)

        @pl.loop(0, spans)
        def _(span):
            entry = spread(entry_ref[span], ones_ref[slot])
            from_state = jnp.dot(
                query_ref[span], state_ref[...].astype(bf16), preferred_element_type=f32
            )
            target = pl.ds(pl.multiple_of(span * SPAN, SPAN), SPAN)
            staged_out[slot, target, :] = (
                staged_out[slot, target, :].astype(f32) + from_state * entry
            ).astype(bf16)
            state_ref[...] = entry[SPAN - 1 :, :] * state_ref[...] + added_ref[slot, span]

        out_copy(chunk).start()

    @pl.loop(0, chunks)
    def _(step):
        @pl.when(step + 2 < chunks)
        def _():
            send_chunk(step + 2)

        take_chunk(step)

        @pl.when(step >= 1)
        def _():
            complete(step - 1)

        @pl.when(step >= 2)
        def _():
            out_copy(step - 2).wait()

        done = 0
        for hop in range(1, hops + 1):
            until = spans * hop // hops

            @pl.loop(done, until)
            def _(span):
                within(step, span)

            done = until
            if hop < hops:
                forward(step, hop)

    complete(chunks - 1)
    for chunk in range(max(0, chunks - 2), chunks):
        out_copy(chunk).wait()
    for chunk in range(max(0, chunks - stage.shape[0]), chunks):
        wait_bytes(stage.at[chunk % stage.shape[0], others], send_sem.at[chunk])
    wait_bytes(small_stage.at[others], send_sem.at[chunks])
    wait_bytes(wanted_runs.at[pl.ds(0, groups - 1)], id_send)

    @pl.when(place < shards - 1)
    def _():
        for hop in range(hops):
            wait_bytes(leaving.at[hop], hop_send.at[hop])


CHUNK_HEADS = 8
STAGES = 3


def fused(source, starts, tokens, keys, query, steps, decay, gain, groups, shards, capacity):
    runs, _, full = tokens.shape
    heads = decay.shape[1]
    spans = runs // RUNS
    head_width = full // heads
    chunks = heads // CHUNK_HEADS
    width = CHUNK_HEADS * head_width
    hops = shards - 1
    slots = groups * capacity
    smem = pl.BlockSpec(memory_space=pltpu.SMEM)
    vmem = pl.BlockSpec(memory_space=pltpu.VMEM)
    dma = pltpu.SemaphoreType.DMA
    small = 3 * LANES
    return pl.pallas_call(
        functools.partial(
            fused_kernel, (groups, shards),
            (capacity, spans, chunks, CHUNK_HEADS, head_width, starts.shape[1]),
        ),
        in_specs=[vmem, smem, ANY, ANY, ANY, ANY, vmem, vmem],
        out_specs=ANY,
        out_shape=jax.ShapeDtypeStruct((runs * SEG, full), bf16),
        scratch_shapes=[
            pltpu.VMEM((1, runs), jnp.int32),
            pltpu.VMEM((groups, 1, runs), jnp.int32),
            pltpu.VMEM((groups, LANES), jnp.int32),
            pltpu.VMEM((1, runs), jnp.int32),
            pltpu.SMEM((groups, LANES), jnp.int32),
            pltpu.SMEM((1, runs), jnp.int32),
            pltpu.VMEM((16, LANES), f32),
            pltpu.VMEM((heads, runs * SEG), bf16),
            pltpu.VMEM((runs, SEG, width), bf16),
            pltpu.VMEM((runs, SEG, small), bf16),
            pltpu.VMEM((STAGES, slots, SEG, width), bf16),
            pltpu.VMEM((slots, SEG, small), bf16),
            pltpu.VMEM((chunks, slots, SEG, width), bf16),
            pltpu.VMEM((slots, SEG, small), bf16),
            pltpu.VMEM((slots, SEG, width), bf16),
            pltpu.VMEM((runs, SEG, width), bf16),
            pltpu.VMEM((2, spans, LANES, width), f32),
            pltpu.VMEM((LANES, width), f32),
            pltpu.VMEM((spans, SPAN, LANES), f32),
            pltpu.VMEM((spans, LANES, SPAN), f32),
            pltpu.VMEM((spans, SPAN, 2 * LANES), bf16),
            pltpu.VMEM((spans, SPAN, 2 * LANES), bf16),
            pltpu.VMEM((spans, LANES, SPAN), bf16),
            pltpu.VMEM((spans, SPAN, LANES), bf16),
            pltpu.VMEM((spans, SPAN, SPAN), f32),
            pltpu.VMEM((16, 2 * LANES), bf16),
            pltpu.VMEM((2, 2 * LANES, width), bf16),
            pltpu.VMEM((SPAN, LANES), f32),
            pltpu.VMEM((16, 2 * LANES), bf16),
            pltpu.VMEM((LANES, width), f32),
            pltpu.VMEM((2, runs * SEG, width), bf16),
            pltpu.VMEM((hops, LANES, width), bf16),
            pltpu.VMEM((chunks, hops, LANES, width), bf16),
            dma((2,)),
            dma,
            dma,
            dma,
            dma((3,)),
            dma((chunks + 1,)),
            dma((chunks + 1,)),
            dma((chunks + 1,)),
            dma,
            dma((hops,)),
            dma((chunks, hops)),
            dma((2,)),
        ],
        compiler_params=params(collective_id=0, has_side_effects=True),
        cost_estimate=pl.CostEstimate(
            flops=8 * runs * SEG * SPAN * full, transcendentals=runs * SEG * SPAN * heads,
            bytes_accessed=4 * runs * SEG * full,
        ),
        name="fused",
    )(source, starts, tokens, keys, query, steps, decay, gain)


def on_device(
    token_rows, key_rows, query_rows, step_rows, decay_log, skip_gain, source_rows, document_starts
):
    tokens, full = token_rows.shape
    groups = lax.axis_size("dp")
    shards = lax.axis_size("seq")
    runs = tokens // SEG
    capacity = runs // groups + 1
    result = fused(
        source_rows, document_starts, token_rows.reshape(runs, SEG, full),
        key_rows.reshape(runs, SEG, LANES), query_rows.reshape(runs, SEG, LANES), step_rows.T,
        decay_log[None, :], skip_gain[None, :], groups, shards, capacity,
    )
    return result[None]


def solution(mesh):
    in_specs = (
        P(("dp", "seq"), None),
        P(("dp", "seq"), None),
        P(("dp", "seq"), None),
        P(("dp", "seq"), None),
        P(),
        P(),
        P("dp", "seq"),
        P("dp", None),
    )
    out_specs = P("dp", "seq", None)
    return jax.shard_map(
        on_device, mesh=mesh, in_specs=in_specs, out_specs=out_specs, check_vma=False
    )
```

```python
import functools

import jax
import jax.numpy as jnp
from jax import lax
from jax.experimental import pallas as pl
from jax.experimental.pallas import tpu as pltpu
from jax.sharding import PartitionSpec as P

SPAN = 256
SEG = 8
RUNS = SPAN // SEG
HALF = SPAN // 2
LANES = 128

f32, bf16 = jnp.float32, jnp.bfloat16
ANY = pl.BlockSpec(memory_space=pl.ANY)
VMEM_LIMIT = 46 * 1024 * 1024


def params(**more):
    return pltpu.CompilerParams(vmem_limit_bytes=VMEM_LIMIT, **more)


def spread(hilo, ones):
    return jnp.dot(hilo, ones, preferred_element_type=f32)


def split_float(value):
    high = value.astype(bf16)
    low = (value - high.astype(f32)).astype(bf16)
    return jnp.concatenate([high, low], axis=1)


def plan_sends(groups, shards, runs, capacity, me, wanted):
    earlier = lax.broadcasted_iota(jnp.int32, (runs, runs), 0) < lax.broadcasted_iota(
        jnp.int32, (runs, runs), 1
    )
    earlier = jnp.where(earlier, 1.0, 0.0).astype(bf16)

    def ranks(hit):
        ones = jnp.where(hit, 1.0, 0.0).astype(bf16)
        return jnp.dot(ones, earlier, preferred_element_type=f32).astype(jnp.int32)

    mine = (wanted // runs) // shards == me
    local = wanted % runs
    rank = ranks(mine)
    lane = lax.broadcasted_iota(jnp.int32, (groups, LANES), 1)
    send = jnp.zeros((groups, LANES), jnp.int32)
    for slot in range(capacity):
        chosen = jnp.sum(jnp.where(mine & (rank == slot), local, 0), axis=1, keepdims=True)
        send = jnp.where(lane == slot, chosen, send)
    return send, ranks


def plan_picks(groups, shards, runs, capacity, own, ranks):
    source = (own // runs) // shards
    group = lax.broadcasted_iota(jnp.int32, (groups, runs), 0)
    hit = jnp.broadcast_to(source, (groups, runs)) == group
    return jnp.sum(jnp.where(hit, group * capacity + ranks(hit), 0), axis=0, keepdims=True)


def fused_kernel(
    axes, sizes, source_ref, starts_ref, tokens_hbm, key_hbm, query_hbm, step_hbm, decay_log_ref, gain_ref, out_ref,
    own_runs, wanted_runs, plan_ref, choice_ref, send_ref, pick_ref, head_ref, turned_steps,
    token, small, stage, small_stage, landing, small_landing, current, values_ref, added_ref, final_ref,
    cum_ref, bias_ref, entry_ref, end_ref, keys_ref, query_ref, score_ref, through_ref,
    ones_ref, turned_ref, skip_ref, state_ref, leaving, entering,
    plan_sem, id_send, id_recv,
    token_sem, small_sem, own_sem, send_sem, recv_sem, current_sem, hop_send, hop_recv,
):
    groups, shards = axes
    capacity, spans, chunks, heads, head_width, starts_count = sizes
    final_chunk = chunks - 1
    pieces = cut_chunk(heads, head_width)
    small_at = final_chunk + len(pieces)
    width = heads * head_width
    hops = shards - 1
    runs = spans * RUNS
    all_heads = chunks * heads
    me = lax.axis_index("dp")
    place = lax.axis_index("seq")

    def token_copy(chunk):
        column = pl.multiple_of(chunk * width, LANES)
        return pltpu.make_async_copy(
            tokens_hbm.at[:, :, pl.ds(column, width)], token, token_sem
        )

    small_parts = [
        pltpu.make_async_copy(key_hbm, small.at[:, :, pl.ds(0, LANES)], small_sem.at[0]),
        pltpu.make_async_copy(query_hbm, small.at[:, :, pl.ds(LANES, LANES)], small_sem.at[1]),
        pltpu.make_async_copy(step_hbm, turned_steps, small_sem.at[2]),
    ]
    token_copy(0).start()
    for part in small_parts:
        part.start()

    barrier = pltpu.get_barrier_semaphore()

    def greet(**device):
        pl.semaphore_signal(barrier, inc=1, device_id=device, device_id_type=pl.DeviceIdType.MESH)

    @pl.when(place == 0)
    def _():
        entering[...] = jnp.zeros_like(entering)

    @pl.loop(1, groups)
    def _(distance):
        greet(dp=lax.rem(me + distance, groups))

    neighbours = 0
    for distance in {1, shards - 1} if shards > 1 else ():
        greet(seq=lax.rem(place + distance, shards))
        neighbours += 1

    every = lax.broadcasted_iota(jnp.int32, (runs * SEG, runs), 0) == SEG * lax.broadcasted_iota(
        jnp.int32, (runs * SEG, runs), 1
    )
    every = jnp.where(every, 1.0, 0.0).astype(bf16)
    numbers = source_ref[...] // SEG
    parts = [((numbers >> shift) & 255).astype(f32).astype(bf16) for shift in (0, 8, 16)]
    own = jnp.dot(
        jnp.concatenate([jnp.broadcast_to(part, (8, runs * SEG)) for part in parts], axis=0), every,
        preferred_element_type=f32,
    ).astype(jnp.int32)
    own = own[0:1] + own[8:9] * 256 + own[16:17] * 65536
    own_runs[...] = own
    wanted_runs[me] = own
    pl.semaphore_wait(barrier, groups - 1 + neighbours)

    @pl.loop(1, groups)
    def _(distance):
        group = lax.rem(me + distance, groups)
        pltpu.make_async_remote_copy(
            src_ref=own_runs, dst_ref=wanted_runs.at[me], send_sem=id_send, recv_sem=id_recv,
            device_id={"dp": group}, device_id_type=pl.DeviceIdType.MESH,
        ).start()

    def wait_bytes(ref, sem):
        pltpu.make_async_copy(ref, ref, sem).wait()

    wait_bytes(wanted_runs.at[pl.ds(0, groups - 1)], id_recv)
    wanted = jnp.concatenate([wanted_runs[group] for group in range(groups)], axis=0)
    plan_ref[...], ranks = plan_sends(groups, shards, runs, capacity, me, wanted)
    plan_copy = pltpu.make_async_copy(plan_ref, send_ref, plan_sem.at[0])
    plan_copy.start()
    choice_ref[...] = plan_picks(groups, shards, runs, capacity, own, ranks)
    choice_copy = pltpu.make_async_copy(choice_ref, pick_ref, plan_sem.at[1])
    choice_copy.start()
    plan_copy.wait()

    def scatter(source, buffer, target, sems, columns=slice(None)):
        own_done, send, recv = sems

        def gather(group):
            start = group * capacity
            for slot in range(capacity):
                buffer[start + slot, :, columns] = source[send_ref[group, slot], :, columns]
            return pl.ds(start, capacity)

        home = pl.ds(me * capacity, capacity)

        @pl.loop(1, groups)
        def _(distance):
            group = lax.rem(me + distance, groups)
            part = gather(group)
            pltpu.make_async_remote_copy(
                src_ref=buffer.at[part, :, columns], dst_ref=target.at[home, :, columns],
                send_sem=send, recv_sem=recv, device_id={"dp": group},
                device_id_type=pl.DeviceIdType.MESH,
            ).start()

        part = gather(me)
        pltpu.make_async_copy(
            buffer.at[part, :, columns], target.at[home, :, columns], own_done
        ).start()

    others = pl.ds(0, (groups - 1) * capacity)
    single = pl.ds(0, capacity)

    def arrived(target, own, recv, columns=slice(None)):
        wait_bytes(target.at[others, :, columns], recv)
        wait_bytes(target.at[single, :, columns], own)

    depth_of_stage = stage.shape[0]

    def ready_to_send(chunk):
        token_copy(chunk).wait()

        @pl.when(chunk >= depth_of_stage)
        def _():
            wait_bytes(
                stage.at[lax.rem(chunk, depth_of_stage), others], send_sem.at[chunk - depth_of_stage]
            )

    def send_chunk(chunk):
        ready_to_send(chunk)
        scatter(
            token, stage.at[lax.rem(chunk, depth_of_stage)], landing.at[chunk],
            (own_sem.at[chunk], send_sem.at[chunk], recv_sem.at[chunk]),
        )
        token_copy(chunk + 1).start()

    def send_pieces():
        ready_to_send(jnp.int32(final_chunk))
        for number, columns in pieces:
            at = final_chunk + number
            scatter(
                token, stage.at[final_chunk % depth_of_stage], landing.at[final_chunk],
                (own_sem.at[at], send_sem.at[at], recv_sem.at[at]), columns,
            )

    send_chunk(0)
    for part in small_parts:
        part.wait()
    steps_across = turned_steps[...].astype(f32)
    steps_across = jnp.concatenate(
        [steps_across, jnp.zeros((LANES - all_heads, runs * SEG), f32)], axis=0
    )
    small[:, :, 2 * LANES :] = steps_across.T.reshape(runs, SEG, LANES).astype(bf16)
    scatter(
        small, small_stage, small_landing,
        (own_sem.at[small_at], send_sem.at[small_at], recv_sem.at[small_at]),
    )
    choice_copy.wait()
    send_chunk(1)
    head_ref[...] = jnp.zeros_like(head_ref)
    head_ref[0:1, :all_heads] = decay_log_ref[...]
    head_ref[8:9, :all_heads] = gain_ref[...]
    skip_ref[...] = split_float(jnp.broadcast_to(head_ref[8:9, :], (16, LANES)))
    arrived(small_landing, own_sem.at[small_at], recv_sem.at[small_at])

    row = lax.broadcasted_iota(jnp.int32, (SPAN, SPAN), 0)
    col = lax.broadcasted_iota(jnp.int32, (SPAN, SPAN), 1)
    row_lanes = lax.broadcasted_iota(jnp.int32, (SPAN, LANES), 0)

    def prepare(span, carry):
        total_before, restarts = carry
        picked = jnp.stack(
            [small_landing[pick_ref[0, span * RUNS + run]].astype(f32) for run in range(RUNS)]
        ).reshape(SPAN, 3 * LANES)
        keys = picked[:, :LANES]
        query = picked[:, LANES : 2 * LANES]
        raw = picked[:, 2 * LANES :]
        steps = jnp.maximum(raw, 0.0) + jnp.log1p(jnp.exp(-jnp.abs(raw)))
        log_decay = -steps * jnp.exp(head_ref[0:1, :])
        lower = jnp.where(col <= row, 1.0, 0.0)
        cum = jnp.dot(lower, log_decay, precision=lax.Precision.HIGHEST, preferred_element_type=f32)
        doc_row = jnp.zeros((SPAN, SPAN), jnp.int32)
        doc_col = jnp.zeros((SPAN, SPAN), jnp.int32)
        doc = jnp.zeros((SPAN, LANES), jnp.int32)
        last = jnp.int32(0)
        for number in range(starts_count):
            start = starts_ref[0, number] - (place * spans + span) * SPAN
            inside = (start >= 0) & (start < SPAN)
            at = jnp.where(inside, start, jnp.int32(1 << 20))
            doc_row += (row >= at).astype(jnp.int32)
            doc_col += (col >= at).astype(jnp.int32)
            doc += (row_lanes >= at).astype(jnp.int32)
            last += inside.astype(jnp.int32)
        linked = (doc_row == doc_col) & (col <= row)
        scores = lax.dot_general(
            query.astype(bf16), keys.astype(bf16), (((1,), (1,)), ((), ())),
            preferred_element_type=f32,
        )
        score_ref[span] = jnp.where(linked, scores, 0.0)
        total = cum[SPAN - 1 :, :]
        entry_ref[span] = split_float(jnp.where(doc == 0, jnp.exp(cum), 0.0))
        end_ref[span] = split_float(jnp.where(doc == last, jnp.exp(total - cum), 0.0) * steps)
        cum_ref[span] = cum
        bias_ref[span] = (jnp.log(steps) - cum).T
        keys_ref[span] = keys.T.astype(bf16)
        query_ref[span] = query.astype(bf16)
        return total_before + total, restarts + last

    total, restarts = lax.fori_loop(
        0, spans, prepare, (jnp.zeros((1, LANES), f32), jnp.int32(0))
    )
    through = jnp.where(restarts == 0, jnp.exp(total), 0.0)
    through_ref[...] = split_float(jnp.broadcast_to(through, (16, LANES)))

    def select_heads(chunk):
        wanted = lax.broadcasted_iota(jnp.int32, (LANES, width), 0) - chunk * heads
        own_head = lax.broadcasted_iota(jnp.int32, (LANES, width), 1) // head_width
        ones = jnp.where(wanted == own_head, 1.0, 0.0).astype(bf16)
        slot = lax.rem(chunk, 2)
        ones_ref[slot, pl.ds(0, LANES), :] = ones
        ones_ref[slot, pl.ds(LANES, LANES), :] = ones

    everything = (0, slice(0, width))

    def span_values(span, columns):
        part = pl.ds(pl.multiple_of(span * RUNS, RUNS), RUNS)
        lanes = columns.stop - columns.start
        return values_ref[part, :, columns].astype(f32).reshape(SPAN, lanes)

    def pass_on(chunk, part, hop, state):
        number, columns = part
        place_left = leaving.at[hop, :, columns]
        at = number if part is everything else 1 + number
        send = hop_send.at[at, hop]

        @pl.when((place < shards - 1) & (chunk > 0) & (part is everything))
        def _():
            wait_bytes(place_left, send)

        @pl.when(place < shards - 1)
        def _():
            leaving[hop, :, columns] = state.astype(bf16)
            pltpu.make_async_remote_copy(
                src_ref=place_left, dst_ref=entering.at[chunk, hop, :, columns],
                send_sem=send, recv_sem=hop_recv.at[chunk + number, hop],
                device_id={"seq": jnp.minimum(place + 1, shards - 1)},
                device_id_type=pl.DeviceIdType.MESH,
            ).start()

    def wait_hop(chunk, part, hop):
        number, columns = part

        @pl.when(place > 0)
        def _():
            wait_bytes(entering.at[chunk, hop, :, columns], hop_recv.at[chunk + number, hop])

    def take(chunk, part):
        number, columns = part
        lanes = columns.stop - columns.start
        slot = lax.rem(chunk, 2)
        at = chunk + number
        arrived(landing.at[chunk], own_sem.at[at], recv_sem.at[at], columns)
        copy = pltpu.make_async_copy(
            landing.at[chunk, :, :, columns], current.at[:, :, columns], current_sem
        )
        copy.start()
        if number == 0:
            select_heads(chunk)
        copy.wait()
        final_ref[:, columns] = jnp.zeros((LANES, lanes), f32)

        @pl.loop(0, spans)
        def _(span):
            for run in range(RUNS):
                picked = pick_ref[0, span * RUNS + run]
                values_ref[span * RUNS + run, :, columns] = current[picked, :, columns]
            ones = ones_ref[slot, :, columns]
            scaled = (span_values(span, columns) * spread(end_ref[span], ones)).astype(bf16)
            added = jnp.dot(keys_ref[span], scaled, preferred_element_type=f32)
            added_ref[slot, span, :, columns] = added
            kept = spread(entry_ref[span, pl.ds(SPAN - 16, 16), :], ones)[15:16, :]
            final_ref[:, columns] = kept * final_ref[:, columns] + added

        pass_on(chunk, part, 0, final_ref[:, columns])

    def forward(chunk, part, hop):
        columns = part[1]
        wait_hop(chunk, part, hop - 1)
        kept = spread(through_ref[...], ones_ref[lax.rem(chunk, 2), :, columns])[0:1, :]
        before = entering[chunk, hop - 1, :, columns].astype(f32)
        pass_on(chunk, part, hop, kept * before + final_ref[:, columns])

    per_tile = LANES // head_width
    lane = lax.broadcasted_iota(jnp.int32, (HALF, LANES), 1) // head_width

    def within(chunk, part, span):
        columns = part[1]
        first_head = pl.multiple_of(chunk * heads, heads)
        values = span_values(span, columns)
        skipped = spread(skip_ref[...], ones_ref[lax.rem(chunk, 2), :, columns])[0:1, :] * values
        turned_ref[...] = pltpu.roll(cum_ref[span], lax.rem(LANES - first_head, LANES), axis=1)
        bias = bias_ref[span, pl.ds(first_head, heads), :]
        packed = values.astype(bf16)
        first_tile = columns.start // LANES
        for tile in range((columns.stop - columns.start) // LANES):
            inside = slice(tile * LANES, (tile + 1) * LANES)
            for half in range(2):
                rows = slice(half * HALF, (half + 1) * HALF)
                depth = (half + 1) * HALF
                scores = score_ref[span, rows, :depth]
                total = None
                for inner in range(per_tile):
                    head = (first_tile + tile) * per_tile + inner
                    gap = turned_ref[rows, head : head + 1] + bias[head : head + 1, :depth]
                    weights = (scores * jnp.exp(jnp.minimum(gap, 60.0))).astype(bf16)
                    piece = jnp.dot(weights, packed[:depth, inside], preferred_element_type=f32)
                    total = piece if total is None else jnp.where(lane == inner, piece, total)
                target = pl.ds(pl.multiple_of(span * SPAN + half * HALF, HALF), HALF)
                column = pl.multiple_of(chunk * width + (first_tile + tile) * LANES, LANES)
                out_ref[target, pl.ds(column, LANES)] = (skipped[rows, inside] + total).astype(bf16)

    def complete(chunk, part):
        columns = part[1]
        lanes = columns.stop - columns.start
        slot = lax.rem(chunk, 2)
        wait_hop(chunk, part, hops - 1)
        state_ref[:, columns] = entering[chunk, hops - 1, :, columns].astype(f32)
        column = pl.multiple_of(chunk * width + columns.start, LANES)

        @pl.loop(0, spans)
        def _(span):
            entry = spread(entry_ref[span], ones_ref[slot, :, columns])
            state = state_ref[:, columns]
            from_state = jnp.dot(query_ref[span], state.astype(bf16), preferred_element_type=f32)
            target = (
                pl.ds(pl.multiple_of(span * SPAN, SPAN), SPAN), pl.ds(column, lanes)
            )
            out_ref[target] = (out_ref[target].astype(f32) + from_state * entry).astype(bf16)
            state_ref[:, columns] = entry[SPAN - 1 :, :] * state + added_ref[slot, span, :, columns]

    @pl.loop(0, final_chunk)
    def _(step):
        @pl.when(step + 2 < final_chunk)
        def _():
            send_chunk(step + 2)

        @pl.when(step + 2 == final_chunk)
        def _():
            send_pieces()

        take(step, everything)

        @pl.when(step >= 1)
        def _():
            complete(step - 1, everything)

        done = 0
        for hop in range(1, hops + 1):
            until = spans * hop // hops

            @pl.loop(done, until)
            def _(span):
                within(step, everything, span)

            done = until
            if hop < hops:
                forward(step, everything, hop)

    @pl.when(place < shards - 1)
    def _():
        for hop in range(hops):
            wait_bytes(leaving.at[hop], hop_send.at[0, hop])

    final = jnp.int32(final_chunk)
    for turn in range(len(pieces) + hops):
        if turn < len(pieces):
            take(final, pieces[turn])
        if turn == 0:
            complete(final - 1, everything)
        for hop in range(2, hops):
            if 0 <= turn - hop + 1 < len(pieces):
                forward(final, pieces[turn - hop + 1], hop)
        if turn < len(pieces):

            @pl.loop(0, spans)
            def _(span):
                within(final, pieces[turn], span)

            if hops > 1:
                forward(final, pieces[turn], 1)
        if 0 <= turn - hops + 1 < len(pieces):
            complete(final, pieces[turn - hops + 1])

    for chunk in range(max(0, chunks - depth_of_stage), final_chunk):
        wait_bytes(stage.at[chunk % depth_of_stage, others], send_sem.at[chunk])
    for number, columns in pieces:
        sent = stage.at[final_chunk % depth_of_stage, others, :, columns]
        wait_bytes(sent, send_sem.at[final_chunk + number])
    wait_bytes(small_stage.at[others], send_sem.at[small_at])
    wait_bytes(wanted_runs.at[pl.ds(0, groups - 1)], id_send)

    @pl.when(place < shards - 1)
    def _():
        for number, columns in pieces:
            for hop in range(hops):
                wait_bytes(leaving.at[hop, :, columns], hop_send.at[1 + number, hop])


def flush_kernel(held_ref, out_ref, sems):
    rows = held_ref.shape[0] // sems.shape[0]
    copies = []
    for number in range(sems.shape[0]):
        part = pl.ds(number * rows, rows)
        copies.append(pltpu.make_async_copy(held_ref.at[part], out_ref.at[part], sems.at[number]))
        copies[-1].start()
    for copy in copies:
        copy.wait()


def flush(held):
    return pl.pallas_call(
        flush_kernel,
        in_specs=[pl.BlockSpec(memory_space=pltpu.VMEM)],
        out_specs=ANY,
        out_shape=jax.ShapeDtypeStruct(held.shape, held.dtype),
        scratch_shapes=[pltpu.SemaphoreType.DMA((FLUSHES,))],
        compiler_params=pltpu.CompilerParams(vmem_limit_bytes=1024 * 1024),
        name="flush",
    )(pltpu.with_memory_space_constraint(held, pltpu.VMEM))


def cut_chunk(heads, head_width):
    pieces, start = [], 0
    for share in CUTS:
        stop = start + heads * head_width * share // sum(CUTS)
        pieces.append((len(pieces), slice(start, stop)))
        start = stop
    return pieces


CUTS = (2, 1, 1)
FLUSHES = 10
CHUNK_HEADS = 8
STAGES = 3


def fused(source, starts, tokens, keys, query, steps, decay, gain, groups, shards, capacity):
    runs, _, full = tokens.shape
    heads = decay.shape[1]
    spans = runs // RUNS
    head_width = full // heads
    chunks = heads // CHUNK_HEADS
    width = CHUNK_HEADS * head_width
    hops = shards - 1
    slots = groups * capacity
    smem = pl.BlockSpec(memory_space=pltpu.SMEM)
    vmem = pl.BlockSpec(memory_space=pltpu.VMEM)
    dma = pltpu.SemaphoreType.DMA
    small = 3 * LANES
    pieces = len(CUTS)
    return pl.pallas_call(
        functools.partial(
            fused_kernel, (groups, shards),
            (capacity, spans, chunks, CHUNK_HEADS, head_width, starts.shape[1]),
        ),
        in_specs=[vmem, smem, ANY, ANY, ANY, ANY, vmem, vmem],
        out_specs=vmem,
        out_shape=pltpu.VMEM((runs * SEG, full), bf16),
        scratch_shapes=[
            pltpu.VMEM((1, runs), jnp.int32),
            pltpu.VMEM((groups, 1, runs), jnp.int32),
            pltpu.VMEM((groups, LANES), jnp.int32),
            pltpu.VMEM((1, runs), jnp.int32),
            pltpu.SMEM((groups, LANES), jnp.int32),
            pltpu.SMEM((1, runs), jnp.int32),
            pltpu.VMEM((16, LANES), f32),
            pltpu.VMEM((heads, runs * SEG), bf16),
            pltpu.VMEM((runs, SEG, width), bf16),
            pltpu.VMEM((runs, SEG, small), bf16),
            pltpu.VMEM((STAGES, slots, SEG, width), bf16),
            pltpu.VMEM((slots, SEG, small), bf16),
            pltpu.VMEM((chunks, slots, SEG, width), bf16),
            pltpu.VMEM((slots, SEG, small), bf16),
            pltpu.VMEM((slots, SEG, width), bf16),
            pltpu.VMEM((runs, SEG, width), bf16),
            pltpu.VMEM((2, spans, LANES, width), f32),
            pltpu.VMEM((LANES, width), f32),
            pltpu.VMEM((spans, SPAN, LANES), f32),
            pltpu.VMEM((spans, LANES, SPAN), f32),
            pltpu.VMEM((spans, SPAN, 2 * LANES), bf16),
            pltpu.VMEM((spans, SPAN, 2 * LANES), bf16),
            pltpu.VMEM((spans, LANES, SPAN), bf16),
            pltpu.VMEM((spans, SPAN, LANES), bf16),
            pltpu.VMEM((spans, SPAN, SPAN), f32),
            pltpu.VMEM((16, 2 * LANES), bf16),
            pltpu.VMEM((2, 2 * LANES, width), bf16),
            pltpu.VMEM((SPAN, LANES), f32),
            pltpu.VMEM((16, 2 * LANES), bf16),
            pltpu.VMEM((LANES, width), f32),
            pltpu.VMEM((hops, LANES, width), bf16),
            pltpu.VMEM((chunks, hops, LANES, width), bf16),
            dma((2,)),
            dma,
            dma,
            dma,
            dma((3,)),
            dma((chunks + pieces,)),
            dma((chunks + pieces,)),
            dma((chunks + pieces,)),
            dma,
            dma((1 + pieces, hops)),
            dma((chunks - 1 + pieces, hops)),
        ],
        compiler_params=params(collective_id=0, has_side_effects=True),
        cost_estimate=pl.CostEstimate(
            flops=8 * runs * SEG * SPAN * full, transcendentals=runs * SEG * SPAN * heads,
            bytes_accessed=4 * runs * SEG * full,
        ),
        name="fused",
    )(source, starts, tokens, keys, query, steps, decay, gain)


def on_device(
    token_rows, key_rows, query_rows, step_rows, decay_log, skip_gain, source_rows, document_starts
):
    tokens, full = token_rows.shape
    groups = lax.axis_size("dp")
    shards = lax.axis_size("seq")
    runs = tokens // SEG
    capacity = runs // groups + 1
    result = fused(
        source_rows, document_starts, token_rows.reshape(runs, SEG, full),
        key_rows.reshape(runs, SEG, LANES), query_rows.reshape(runs, SEG, LANES), step_rows.T,
        decay_log[None, :], skip_gain[None, :], groups, shards, capacity,
    )
    return flush(result)[None]


def solution(mesh):
    in_specs = (
        P(("dp", "seq"), None),
        P(("dp", "seq"), None),
        P(("dp", "seq"), None),
        P(("dp", "seq"), None),
        P(),
        P(),
        P("dp", "seq"),
        P("dp", None),
    )
    out_specs = P("dp", "seq", None)
    return jax.shard_map(
        on_device, mesh=mesh, in_specs=in_specs, out_specs=out_specs, check_vma=False
    )
```

```python
import functools

import jax
import jax.numpy as jnp
from jax import lax
from jax.experimental import pallas as pl
from jax.experimental.pallas import tpu as pltpu
from jax.sharding import PartitionSpec as P

SPAN = 256
SEG = 8
RUNS = SPAN // SEG
HALF = SPAN // 2
LANES = 128

f32, bf16 = jnp.float32, jnp.bfloat16
ANY = pl.BlockSpec(memory_space=pl.ANY)
VMEM_LIMIT = 46 * 1024 * 1024


def params(**more):
    return pltpu.CompilerParams(vmem_limit_bytes=VMEM_LIMIT, **more)


def spread(hilo, ones):
    return jnp.dot(hilo, ones, preferred_element_type=f32)


def split_float(value):
    high = value.astype(bf16)
    low = (value - high.astype(f32)).astype(bf16)
    return jnp.concatenate([high, low], axis=1)


def plan_sends(groups, shards, runs, capacity, me, wanted):
    earlier = lax.broadcasted_iota(jnp.int32, (runs, runs), 0) < lax.broadcasted_iota(
        jnp.int32, (runs, runs), 1
    )
    earlier = jnp.where(earlier, 1.0, 0.0).astype(bf16)

    def ranks(hit):
        ones = jnp.where(hit, 1.0, 0.0).astype(bf16)
        return jnp.dot(ones, earlier, preferred_element_type=f32).astype(jnp.int32)

    mine = (wanted // runs) // shards == me
    local = wanted % runs
    rank = ranks(mine)
    lane = lax.broadcasted_iota(jnp.int32, (groups, LANES), 1)
    send = jnp.zeros((groups, LANES), jnp.int32)
    for slot in range(capacity):
        chosen = jnp.sum(jnp.where(mine & (rank == slot), local, 0), axis=1, keepdims=True)
        send = jnp.where(lane == slot, chosen, send)
    return send, ranks


def plan_picks(groups, shards, runs, capacity, own, ranks):
    source = (own // runs) // shards
    group = lax.broadcasted_iota(jnp.int32, (groups, runs), 0)
    hit = jnp.broadcast_to(source, (groups, runs)) == group
    return jnp.sum(jnp.where(hit, group * capacity + ranks(hit), 0), axis=0, keepdims=True)


def fused_kernel(
    axes, sizes, source_ref, starts_ref, tokens_hbm, key_hbm, query_hbm, step_hbm, decay_log_ref, gain_ref, out_ref,
    own_runs, wanted_runs, plan_ref, choice_ref, send_ref, pick_ref, head_ref, turned_steps,
    token, small, stage, small_stage, landing, small_landing, current, values_ref, added_ref, final_ref,
    cum_ref, bias_ref, entry_ref, end_ref, keys_ref, query_ref, score_ref, through_ref,
    ones_ref, turned_ref, skip_ref, state_ref, leaving, entering,
    plan_sem, id_send, id_recv,
    token_sem, small_sem, own_sem, send_sem, recv_sem, current_sem, hop_send, hop_recv,
):
    groups, shards = axes
    capacity, spans, chunks, heads, head_width, starts_count = sizes
    ring = hops_of(shards) + 1
    small_at = chunks
    width = heads * head_width
    hops = hops_of(shards)
    runs = spans * RUNS
    all_heads = chunks * heads
    me = lax.axis_index("dp")
    place = lax.axis_index("seq")

    def token_copy(chunk):
        column = pl.multiple_of(chunk * width, LANES)
        return pltpu.make_async_copy(
            tokens_hbm.at[:, :, pl.ds(column, width)], token, token_sem
        )

    small_parts = [
        pltpu.make_async_copy(key_hbm, small.at[:, :, pl.ds(0, LANES)], small_sem.at[0]),
        pltpu.make_async_copy(query_hbm, small.at[:, :, pl.ds(LANES, LANES)], small_sem.at[1]),
        pltpu.make_async_copy(step_hbm, turned_steps, small_sem.at[2]),
    ]
    token_copy(0).start()
    for part in small_parts:
        part.start()

    barrier = pltpu.get_barrier_semaphore()

    def greet(**device):
        pl.semaphore_signal(barrier, inc=1, device_id=device, device_id_type=pl.DeviceIdType.MESH)

    @pl.loop(1, groups)
    def _(distance):
        greet(dp=lax.rem(me + distance, groups))

    neighbours = 0
    for distance in {1, shards - 1} if shards > 1 else ():
        greet(seq=lax.rem(place + distance, shards))
        neighbours += 1

    every = lax.broadcasted_iota(jnp.int32, (runs * SEG, runs), 0) == SEG * lax.broadcasted_iota(
        jnp.int32, (runs * SEG, runs), 1
    )
    every = jnp.where(every, 1.0, 0.0).astype(bf16)
    numbers = source_ref[...] // SEG
    parts = [((numbers >> shift) & 255).astype(f32).astype(bf16) for shift in (0, 8, 16)]
    own = jnp.dot(
        jnp.concatenate([jnp.broadcast_to(part, (8, runs * SEG)) for part in parts], axis=0), every,
        preferred_element_type=f32,
    ).astype(jnp.int32)
    own = own[0:1] + own[8:9] * 256 + own[16:17] * 65536
    own_runs[...] = own
    wanted_runs[me] = own
    pl.semaphore_wait(barrier, groups - 1 + neighbours)

    @pl.loop(1, groups)
    def _(distance):
        group = lax.rem(me + distance, groups)
        pltpu.make_async_remote_copy(
            src_ref=own_runs, dst_ref=wanted_runs.at[me], send_sem=id_send, recv_sem=id_recv,
            device_id={"dp": group}, device_id_type=pl.DeviceIdType.MESH,
        ).start()

    def wait_bytes(ref, sem):
        pltpu.make_async_copy(ref, ref, sem).wait()

    wait_bytes(wanted_runs.at[pl.ds(0, groups - 1)], id_recv)
    wanted = jnp.concatenate([wanted_runs[group] for group in range(groups)], axis=0)
    plan_ref[...], ranks = plan_sends(groups, shards, runs, capacity, me, wanted)
    plan_copy = pltpu.make_async_copy(plan_ref, send_ref, plan_sem.at[0])
    plan_copy.start()
    choice_ref[...] = plan_picks(groups, shards, runs, capacity, own, ranks)
    choice_copy = pltpu.make_async_copy(choice_ref, pick_ref, plan_sem.at[1])
    choice_copy.start()
    plan_copy.wait()

    def scatter(source, buffer, target, sems):
        own_done, send, recv = sems

        def gather(group):
            start = group * capacity
            for slot in range(capacity):
                buffer[start + slot] = source[send_ref[group, slot]]
            return pl.ds(start, capacity)

        home = pl.ds(me * capacity, capacity)

        @pl.loop(1, groups)
        def _(distance):
            group = lax.rem(me + distance, groups)
            part = gather(group)
            pltpu.make_async_remote_copy(
                src_ref=buffer.at[part], dst_ref=target.at[home],
                send_sem=send, recv_sem=recv, device_id={"dp": group},
                device_id_type=pl.DeviceIdType.MESH,
            ).start()

        part = gather(me)
        pltpu.make_async_copy(
            buffer.at[part], target.at[home], own_done
        ).start()

    others = pl.ds(0, (groups - 1) * capacity)
    single = pl.ds(0, capacity)

    def arrived(target, own, recv):
        wait_bytes(target.at[others], recv)
        wait_bytes(target.at[single], own)

    stages = stage.shape[0]

    def send_chunk(chunk):
        slot = lax.rem(chunk, stages)
        token_copy(chunk).wait()

        @pl.when(chunk >= stages)
        def _():
            wait_bytes(stage.at[slot, others], send_sem.at[chunk - stages])

        scatter(
            token, stage.at[slot], landing.at[chunk],
            (own_sem.at[chunk], send_sem.at[chunk], recv_sem.at[chunk]),
        )

        @pl.when(chunk + 1 < chunks)
        def _():
            token_copy(chunk + 1).start()

    send_chunk(jnp.int32(0))
    for part in small_parts:
        part.wait()
    steps_across = turned_steps[...].astype(f32)
    steps_across = jnp.concatenate(
        [steps_across, jnp.zeros((LANES - all_heads, runs * SEG), f32)], axis=0
    )
    small[:, :, 2 * LANES :] = steps_across.T.reshape(runs, SEG, LANES).astype(bf16)
    scatter(
        small, small_stage, small_landing,
        (own_sem.at[small_at], send_sem.at[small_at], recv_sem.at[small_at]),
    )
    choice_copy.wait()
    @pl.loop(1, AHEAD)
    def _(chunk):
        send_chunk(chunk)

    head_ref[...] = jnp.zeros_like(head_ref)
    head_ref[0:1, :all_heads] = decay_log_ref[...]
    head_ref[8:9, :all_heads] = gain_ref[...]
    skip_ref[...] = split_float(jnp.broadcast_to(head_ref[8:9, :], (16, LANES)))
    arrived(small_landing, own_sem.at[small_at], recv_sem.at[small_at])

    row = lax.broadcasted_iota(jnp.int32, (SPAN, SPAN), 0)
    col = lax.broadcasted_iota(jnp.int32, (SPAN, SPAN), 1)
    row_lanes = lax.broadcasted_iota(jnp.int32, (SPAN, LANES), 0)

    def prepare(span, carry):
        total_before, restarts = carry
        picked = jnp.stack(
            [small_landing[pick_ref[0, span * RUNS + run]].astype(f32) for run in range(RUNS)]
        ).reshape(SPAN, 3 * LANES)
        keys = picked[:, :LANES]
        query = picked[:, LANES : 2 * LANES]
        raw = picked[:, 2 * LANES :]
        steps = jnp.maximum(raw, 0.0) + jnp.log1p(jnp.exp(-jnp.abs(raw)))
        log_decay = -steps * jnp.exp(head_ref[0:1, :])
        lower = jnp.where(col <= row, 1.0, 0.0)
        cum = jnp.dot(lower, log_decay, precision=lax.Precision.HIGHEST, preferred_element_type=f32)
        doc_row = jnp.zeros((SPAN, SPAN), jnp.int32)
        doc_col = jnp.zeros((SPAN, SPAN), jnp.int32)
        doc = jnp.zeros((SPAN, LANES), jnp.int32)
        last = jnp.int32(0)
        for number in range(starts_count):
            start = starts_ref[0, number] - (place * spans + span) * SPAN
            inside = (start >= 0) & (start < SPAN)
            at = jnp.where(inside, start, jnp.int32(1 << 20))
            doc_row += (row >= at).astype(jnp.int32)
            doc_col += (col >= at).astype(jnp.int32)
            doc += (row_lanes >= at).astype(jnp.int32)
            last += inside.astype(jnp.int32)
        linked = (doc_row == doc_col) & (col <= row)
        scores = lax.dot_general(
            query.astype(bf16), keys.astype(bf16), (((1,), (1,)), ((), ())),
            preferred_element_type=f32,
        )
        score_ref[span] = jnp.where(linked, scores, 0.0)
        total = cum[SPAN - 1 :, :]
        entry_ref[span] = split_float(jnp.where(doc == 0, jnp.exp(cum), 0.0))
        end_ref[span] = split_float(jnp.where(doc == last, jnp.exp(total - cum), 0.0) * steps)
        cum_ref[span] = cum
        bias = (jnp.log(steps) - cum).T
        for chunk in range(chunks):
            bias_ref[span, chunk] = bias[chunk * heads : (chunk + 1) * heads]
        keys_ref[span] = keys.T.astype(bf16)
        query_ref[span] = query.astype(bf16)
        return total_before + total, restarts + last

    total, restarts = lax.fori_loop(
        0, spans, prepare, (jnp.zeros((1, LANES), f32), jnp.int32(0))
    )
    through = jnp.where(restarts == 0, jnp.exp(total), 0.0)
    through_ref[...] = split_float(jnp.broadcast_to(through, (16, LANES)))

    def select_heads(chunk):
        wanted = lax.broadcasted_iota(jnp.int32, (LANES, width), 0) - chunk * heads
        own_head = lax.broadcasted_iota(jnp.int32, (LANES, width), 1) // head_width
        ones = jnp.where(wanted == own_head, 1.0, 0.0).astype(bf16)
        slot = lax.rem(chunk, ring)
        ones_ref[slot, pl.ds(0, LANES), :] = ones
        ones_ref[slot, pl.ds(LANES, LANES), :] = ones

    def span_values(span):
        part = pl.ds(pl.multiple_of(span * RUNS, RUNS), RUNS)
        return values_ref[part].astype(f32).reshape(SPAN, width)

    def pass_on(chunk, hop, state):
        slot = lax.rem(chunk, 2)
        left, send = leaving.at[slot, hop], hop_send.at[slot, hop]

        @pl.when((place < shards - 1) & (chunk > 1))
        def _():
            wait_bytes(left, send)

        @pl.when(place < shards - 1)
        def _():
            leaving[slot, hop] = state.astype(bf16)
            pltpu.make_async_remote_copy(
                src_ref=left, dst_ref=entering.at[chunk, hop], send_sem=send,
                recv_sem=hop_recv.at[chunk, hop], device_id={"seq": jnp.minimum(place + 1, shards - 1)},
                device_id_type=pl.DeviceIdType.MESH,
            ).start()

    def handed(chunk, hop):
        @pl.when(place > 0)
        def _():
            wait_bytes(entering.at[chunk, hop], hop_recv.at[chunk, hop])

        return jnp.where(place > 0, entering[chunk, hop].astype(f32), 0.0)

    def take(chunk):
        slot = lax.rem(chunk, ring)
        arrived(landing.at[chunk], own_sem.at[chunk], recv_sem.at[chunk])
        copy = pltpu.make_async_copy(landing.at[chunk], current, current_sem)
        copy.start()

        @pl.when(chunk + AHEAD < chunks)
        def _():
            send_chunk(chunk + AHEAD)

        select_heads(chunk)
        copy.wait()
        final_ref[slot] = jnp.zeros((LANES, width), f32)

        @pl.loop(0, spans)
        def _(span):
            for run in range(RUNS):
                values_ref[span * RUNS + run] = current[pick_ref[0, span * RUNS + run]]
            ones = ones_ref[slot]
            scaled = (span_values(span) * spread(end_ref[span], ones)).astype(bf16)
            added = jnp.dot(keys_ref[span], scaled, preferred_element_type=f32)
            added_ref[slot, span] = added
            kept = spread(entry_ref[span, SPAN - 16 :, :], ones)[15:16, :]
            final_ref[slot] = kept * final_ref[slot] + added

        pass_on(chunk, 0, final_ref[slot])

    def forward(chunk, hop):
        slot = lax.rem(chunk, ring)
        before = handed(chunk, hop - 1)
        kept = spread(through_ref[...], ones_ref[slot])[0:1, :]
        pass_on(chunk, hop, kept * before + final_ref[slot])

    per_tile = LANES // head_width
    lane = lax.broadcasted_iota(jnp.int32, (HALF, LANES), 1) // head_width

    def within(chunk, span):
        values = span_values(span)
        skipped = spread(skip_ref[...], ones_ref[lax.rem(chunk, ring)])[0:1, :] * values
        turn = lax.rem(LANES - chunk * heads, LANES)
        turned_ref[...] = pltpu.roll(cum_ref[span], turn, axis=1)
        bias = bias_ref[span, chunk]
        packed = values.astype(bf16)
        for tile in range(width // LANES):
            inside = slice(tile * LANES, (tile + 1) * LANES)
            for half in range(2):
                rows = slice(half * HALF, (half + 1) * HALF)
                depth = (half + 1) * HALF
                scores = score_ref[span, rows, :depth]
                total = None
                for inner in range(per_tile):
                    head = tile * per_tile + inner
                    gap = turned_ref[rows, head : head + 1] + bias[head : head + 1, :depth]
                    weights = (scores * jnp.exp(jnp.minimum(gap, 60.0))).astype(bf16)
                    piece = jnp.dot(weights, packed[:depth, inside], preferred_element_type=f32)
                    total = piece if total is None else jnp.where(lane == inner, piece, total)
                target = pl.ds(pl.multiple_of(span * SPAN + half * HALF, HALF), HALF)
                column = pl.multiple_of(chunk * width + tile * LANES, LANES)
                out_ref[target, pl.ds(column, LANES)] = (skipped[rows, inside] + total).astype(bf16)

    def complete(chunk):
        slot = lax.rem(chunk, ring)
        state_ref[...] = handed(chunk, hops - 1)
        column = pl.multiple_of(chunk * width, LANES)

        @pl.loop(0, spans)
        def _(span):
            entry = spread(entry_ref[span], ones_ref[slot])
            state = state_ref[...]
            from_state = jnp.dot(query_ref[span], state.astype(bf16), preferred_element_type=f32)
            target = (pl.ds(pl.multiple_of(span * SPAN, SPAN), SPAN), pl.ds(column, width))
            out_ref[target] = (out_ref[target].astype(f32) + from_state * entry).astype(bf16)
            state_ref[...] = entry[SPAN - 1 :, :] * state + added_ref[slot, span]

    @pl.loop(0, chunks + hops)
    def _(step):
        for hop in range(1, hops):

            @pl.when((step >= hop) & (step - hop < chunks))
            def _():
                forward(step - hop, hop)

        @pl.when(step >= hops)
        def _():
            complete(step - hops)

        @pl.when(step < chunks)
        def _():
            take(step)

            @pl.loop(0, spans)
            def _(span):
                within(step, span)

    @pl.loop(chunks - stages, chunks)
    def _(chunk):
        wait_bytes(stage.at[lax.rem(chunk, stages), others], send_sem.at[chunk])

    wait_bytes(small_stage.at[others], send_sem.at[small_at])
    wait_bytes(wanted_runs.at[pl.ds(0, groups - 1)], id_send)

    @pl.when(place < shards - 1)
    def _():
        for slot in range(2):
            for hop in range(hops):
                wait_bytes(leaving.at[slot, hop], hop_send.at[slot, hop])


def flush_kernel(held_ref, out_ref, sems):
    rows = held_ref.shape[0] // sems.shape[0]
    copies = []
    for number in range(sems.shape[0]):
        part = pl.ds(number * rows, rows)
        copies.append(pltpu.make_async_copy(held_ref.at[part], out_ref.at[part], sems.at[number]))
        copies[-1].start()
    for copy in copies:
        copy.wait()


def flush(held):
    return pl.pallas_call(
        flush_kernel,
        in_specs=[pl.BlockSpec(memory_space=pltpu.VMEM)],
        out_specs=ANY,
        out_shape=jax.ShapeDtypeStruct(held.shape, held.dtype),
        scratch_shapes=[pltpu.SemaphoreType.DMA((FLUSHES,))],
        compiler_params=pltpu.CompilerParams(vmem_limit_bytes=1024 * 1024),
        name="flush",
    )(pltpu.with_memory_space_constraint(held, pltpu.VMEM))


def hops_of(shards):
    return shards - 1


AHEAD = 2
FLUSHES = 10
CHUNK_HEADS = 4
STAGES = 4


def fused(source, starts, tokens, keys, query, steps, decay, gain, groups, shards, capacity):
    runs, _, full = tokens.shape
    heads = decay.shape[1]
    spans = runs // RUNS
    head_width = full // heads
    chunks = heads // CHUNK_HEADS
    width = CHUNK_HEADS * head_width
    hops = shards - 1
    slots = groups * capacity
    smem = pl.BlockSpec(memory_space=pltpu.SMEM)
    vmem = pl.BlockSpec(memory_space=pltpu.VMEM)
    dma = pltpu.SemaphoreType.DMA
    small = 3 * LANES
    ring = hops + 1
    return pl.pallas_call(
        functools.partial(
            fused_kernel, (groups, shards),
            (capacity, spans, chunks, CHUNK_HEADS, head_width, starts.shape[1]),
        ),
        in_specs=[vmem, smem, ANY, ANY, ANY, ANY, vmem, vmem],
        out_specs=vmem,
        out_shape=pltpu.VMEM((runs * SEG, full), bf16),
        scratch_shapes=[
            pltpu.VMEM((1, runs), jnp.int32),
            pltpu.VMEM((groups, 1, runs), jnp.int32),
            pltpu.VMEM((groups, LANES), jnp.int32),
            pltpu.VMEM((1, runs), jnp.int32),
            pltpu.SMEM((groups, LANES), jnp.int32),
            pltpu.SMEM((1, runs), jnp.int32),
            pltpu.VMEM((16, LANES), f32),
            pltpu.VMEM((heads, runs * SEG), bf16),
            pltpu.VMEM((runs, SEG, width), bf16),
            pltpu.VMEM((runs, SEG, small), bf16),
            pltpu.VMEM((STAGES, slots, SEG, width), bf16),
            pltpu.VMEM((slots, SEG, small), bf16),
            pltpu.VMEM((chunks, slots, SEG, width), bf16),
            pltpu.VMEM((slots, SEG, small), bf16),
            pltpu.VMEM((slots, SEG, width), bf16),
            pltpu.VMEM((runs, SEG, width), bf16),
            pltpu.VMEM((ring, spans, LANES, width), f32),
            pltpu.VMEM((ring, LANES, width), f32),
            pltpu.VMEM((spans, SPAN, LANES), f32),
            pltpu.VMEM((spans, chunks, CHUNK_HEADS, SPAN), f32),
            pltpu.VMEM((spans, SPAN, 2 * LANES), bf16),
            pltpu.VMEM((spans, SPAN, 2 * LANES), bf16),
            pltpu.VMEM((spans, LANES, SPAN), bf16),
            pltpu.VMEM((spans, SPAN, LANES), bf16),
            pltpu.VMEM((spans, SPAN, SPAN), f32),
            pltpu.VMEM((16, 2 * LANES), bf16),
            pltpu.VMEM((ring, 2 * LANES, width), bf16),
            pltpu.VMEM((SPAN, LANES), f32),
            pltpu.VMEM((16, 2 * LANES), bf16),
            pltpu.VMEM((LANES, width), f32),
            pltpu.VMEM((2, hops, LANES, width), bf16),
            pltpu.VMEM((chunks, hops, LANES, width), bf16),
            dma((2,)),
            dma,
            dma,
            dma,
            dma((3,)),
            dma((chunks + 1,)),
            dma((chunks + 1,)),
            dma((chunks + 1,)),
            dma,
            dma((2, hops)),
            dma((chunks, hops)),
        ],
        compiler_params=params(collective_id=0, has_side_effects=True),
        cost_estimate=pl.CostEstimate(
            flops=8 * runs * SEG * SPAN * full, transcendentals=runs * SEG * SPAN * heads,
            bytes_accessed=4 * runs * SEG * full,
        ),
        name="fused",
    )(source, starts, tokens, keys, query, steps, decay, gain)


def on_device(
    token_rows, key_rows, query_rows, step_rows, decay_log, skip_gain, source_rows, document_starts
):
    tokens, full = token_rows.shape
    groups = lax.axis_size("dp")
    shards = lax.axis_size("seq")
    runs = tokens // SEG
    capacity = runs // groups + 1
    result = fused(
        source_rows, document_starts, token_rows.reshape(runs, SEG, full),
        key_rows.reshape(runs, SEG, LANES), query_rows.reshape(runs, SEG, LANES), step_rows.T,
        decay_log[None, :], skip_gain[None, :], groups, shards, capacity,
    )
    return flush(result)[None]


def solution(mesh):
    in_specs = (
        P(("dp", "seq"), None),
        P(("dp", "seq"), None),
        P(("dp", "seq"), None),
        P(("dp", "seq"), None),
        P(),
        P(),
        P("dp", "seq"),
        P("dp", None),
    )
    out_specs = P("dp", "seq", None)
    return jax.shard_map(
        on_device, mesh=mesh, in_specs=in_specs, out_specs=out_specs, check_vma=False
    )
```

```python
import functools

import jax
import jax.numpy as jnp
from jax import lax
from jax.experimental import pallas as pl
from jax.experimental.pallas import tpu as pltpu
from jax.sharding import PartitionSpec as P

SPAN = 256
SEG = 8
RUNS = SPAN // SEG
HALF = SPAN // 2
LANES = 128

f32, bf16 = jnp.float32, jnp.bfloat16
ANY = pl.BlockSpec(memory_space=pl.ANY)
VMEM_LIMIT = 46 * 1024 * 1024


def params(**more):
    return pltpu.CompilerParams(vmem_limit_bytes=VMEM_LIMIT, **more)


def spread(hilo, ones):
    return jnp.dot(hilo, ones, preferred_element_type=f32)


def split_float(value):
    high = value.astype(bf16)
    low = (value - high.astype(f32)).astype(bf16)
    return jnp.concatenate([high, low], axis=1)


def plan_sends(groups, shards, runs, capacity, me, wanted):
    earlier = lax.broadcasted_iota(jnp.int32, (runs, runs), 0) < lax.broadcasted_iota(
        jnp.int32, (runs, runs), 1
    )
    earlier = jnp.where(earlier, 1.0, 0.0).astype(bf16)

    def ranks(hit):
        ones = jnp.where(hit, 1.0, 0.0).astype(bf16)
        return jnp.dot(ones, earlier, preferred_element_type=f32).astype(jnp.int32)

    mine = (wanted // runs) // shards == me
    local = wanted % runs
    rank = ranks(mine)
    lane = lax.broadcasted_iota(jnp.int32, (groups, LANES), 1)
    send = jnp.zeros((groups, LANES), jnp.int32)
    for slot in range(capacity):
        chosen = jnp.sum(jnp.where(mine & (rank == slot), local, 0), axis=1, keepdims=True)
        send = jnp.where(lane == slot, chosen, send)
    return send, ranks


def plan_picks(groups, shards, runs, capacity, own, ranks):
    source = (own // runs) // shards
    group = lax.broadcasted_iota(jnp.int32, (groups, runs), 0)
    hit = jnp.broadcast_to(source, (groups, runs)) == group
    return jnp.sum(jnp.where(hit, group * capacity + ranks(hit), 0), axis=0, keepdims=True)


def fused_kernel(
    axes, sizes, source_ref, starts_ref, tokens_hbm, key_hbm, query_hbm, step_hbm, decay_log_ref, gain_ref, out_ref,
    own_runs, wanted_runs, plan_ref, choice_ref, send_ref, pick_ref, head_ref, turned_steps,
    token, small, stage, small_stage, landing, small_landing, current, values_ref, added_ref, final_ref,
    cum_ref, bias_ref, entry_ref, end_ref, keys_ref, query_ref, score_ref, through_ref,
    ones_ref, turned_ref, skip_ref, state_ref, leaving, entering, far, far_scale, throughs,
    plan_sem, id_send, id_recv,
    token_sem, small_sem, own_sem, send_sem, recv_sem, current_sem, hop_send, hop_recv, far_send, far_recv, through_send, through_recv,
):
    groups, shards = axes
    capacity, spans, chunks, heads, head_width, starts_count = sizes
    ring = hops_of(shards) + 1
    small_at = chunks
    width = heads * head_width
    hops = hops_of(shards)
    runs = spans * RUNS
    all_heads = chunks * heads
    me = lax.axis_index("dp")
    place = lax.axis_index("seq")

    def token_copy(chunk):
        column = pl.multiple_of(chunk * width, LANES)
        return pltpu.make_async_copy(
            tokens_hbm.at[:, :, pl.ds(column, width)], token, token_sem
        )

    small_parts = [
        pltpu.make_async_copy(key_hbm, small.at[:, :, pl.ds(0, LANES)], small_sem.at[0]),
        pltpu.make_async_copy(query_hbm, small.at[:, :, pl.ds(LANES, LANES)], small_sem.at[1]),
        pltpu.make_async_copy(step_hbm, turned_steps, small_sem.at[2]),
    ]
    token_copy(0).start()
    for part in small_parts:
        part.start()

    barrier = pltpu.get_barrier_semaphore()

    def greet(**device):
        pl.semaphore_signal(barrier, inc=1, device_id=device, device_id_type=pl.DeviceIdType.MESH)

    @pl.loop(1, groups)
    def _(distance):
        greet(dp=lax.rem(me + distance, groups))

    @pl.loop(1, shards)
    def _(distance):
        greet(seq=lax.rem(place + distance, shards))

    every = lax.broadcasted_iota(jnp.int32, (runs * SEG, runs), 0) == SEG * lax.broadcasted_iota(
        jnp.int32, (runs * SEG, runs), 1
    )
    every = jnp.where(every, 1.0, 0.0).astype(bf16)
    numbers = source_ref[...] // SEG
    parts = [((numbers >> shift) & 255).astype(f32).astype(bf16) for shift in (0, 8, 16)]
    own = jnp.dot(
        jnp.concatenate([jnp.broadcast_to(part, (8, runs * SEG)) for part in parts], axis=0), every,
        preferred_element_type=f32,
    ).astype(jnp.int32)
    own = own[0:1] + own[8:9] * 256 + own[16:17] * 65536
    own_runs[...] = own
    wanted_runs[me] = own
    pl.semaphore_wait(barrier, groups - 1 + shards - 1)

    @pl.loop(1, groups)
    def _(distance):
        group = lax.rem(me + distance, groups)
        pltpu.make_async_remote_copy(
            src_ref=own_runs, dst_ref=wanted_runs.at[me], send_sem=id_send, recv_sem=id_recv,
            device_id={"dp": group}, device_id_type=pl.DeviceIdType.MESH,
        ).start()

    def wait_bytes(ref, sem):
        pltpu.make_async_copy(ref, ref, sem).wait()

    wait_bytes(wanted_runs.at[pl.ds(0, groups - 1)], id_recv)
    wanted = jnp.concatenate([wanted_runs[group] for group in range(groups)], axis=0)
    plan_ref[...], ranks = plan_sends(groups, shards, runs, capacity, me, wanted)
    plan_copy = pltpu.make_async_copy(plan_ref, send_ref, plan_sem.at[0])
    plan_copy.start()
    choice_ref[...] = plan_picks(groups, shards, runs, capacity, own, ranks)
    choice_copy = pltpu.make_async_copy(choice_ref, pick_ref, plan_sem.at[1])
    choice_copy.start()
    plan_copy.wait()

    def scatter(source, buffer, target, sems):
        own_done, send, recv = sems

        def gather(group):
            start = group * capacity
            for slot in range(capacity):
                buffer[start + slot] = source[send_ref[group, slot]]
            return pl.ds(start, capacity)

        home = pl.ds(me * capacity, capacity)

        @pl.loop(1, groups)
        def _(distance):
            group = lax.rem(me + distance, groups)
            part = gather(group)
            pltpu.make_async_remote_copy(
                src_ref=buffer.at[part], dst_ref=target.at[home],
                send_sem=send, recv_sem=recv, device_id={"dp": group},
                device_id_type=pl.DeviceIdType.MESH,
            ).start()

        part = gather(me)
        pltpu.make_async_copy(
            buffer.at[part], target.at[home], own_done
        ).start()

    others = pl.ds(0, (groups - 1) * capacity)
    single = pl.ds(0, capacity)

    def arrived(target, own, recv):
        wait_bytes(target.at[others], recv)
        wait_bytes(target.at[single], own)

    stages = stage.shape[0]

    def send_chunk(chunk):
        slot = lax.rem(chunk, stages)
        token_copy(chunk).wait()

        @pl.when(chunk >= stages)
        def _():
            wait_bytes(stage.at[slot, others], send_sem.at[chunk - stages])

        scatter(
            token, stage.at[slot], landing.at[chunk],
            (own_sem.at[chunk], send_sem.at[chunk], recv_sem.at[chunk]),
        )

        @pl.when(chunk + 1 < chunks)
        def _():
            token_copy(chunk + 1).start()

    send_chunk(jnp.int32(0))
    for part in small_parts:
        part.wait()
    steps_across = turned_steps[...].astype(f32)
    steps_across = jnp.concatenate(
        [steps_across, jnp.zeros((LANES - all_heads, runs * SEG), f32)], axis=0
    )
    small[:, :, 2 * LANES :] = steps_across.T.reshape(runs, SEG, LANES).astype(bf16)
    scatter(
        small, small_stage, small_landing,
        (own_sem.at[small_at], send_sem.at[small_at], recv_sem.at[small_at]),
    )
    choice_copy.wait()
    @pl.loop(1, AHEAD)
    def _(chunk):
        send_chunk(chunk)

    head_ref[...] = jnp.zeros_like(head_ref)
    head_ref[0:1, :all_heads] = decay_log_ref[...]
    head_ref[8:9, :all_heads] = gain_ref[...]
    skip_ref[...] = split_float(jnp.broadcast_to(head_ref[8:9, :], (16, LANES)))
    arrived(small_landing, own_sem.at[small_at], recv_sem.at[small_at])

    row = lax.broadcasted_iota(jnp.int32, (SPAN, SPAN), 0)
    col = lax.broadcasted_iota(jnp.int32, (SPAN, SPAN), 1)
    row_lanes = lax.broadcasted_iota(jnp.int32, (SPAN, LANES), 0)

    def prepare(span, carry):
        total_before, restarts = carry
        picked = jnp.stack(
            [small_landing[pick_ref[0, span * RUNS + run]].astype(f32) for run in range(RUNS)]
        ).reshape(SPAN, 3 * LANES)
        keys = picked[:, :LANES]
        query = picked[:, LANES : 2 * LANES]
        raw = picked[:, 2 * LANES :]
        steps = jnp.maximum(raw, 0.0) + jnp.log1p(jnp.exp(-jnp.abs(raw)))
        log_decay = -steps * jnp.exp(head_ref[0:1, :])
        lower = jnp.where(col <= row, 1.0, 0.0)
        cum = jnp.dot(lower, log_decay, precision=lax.Precision.HIGHEST, preferred_element_type=f32)
        doc_row = jnp.zeros((SPAN, SPAN), jnp.int32)
        doc_col = jnp.zeros((SPAN, SPAN), jnp.int32)
        doc = jnp.zeros((SPAN, LANES), jnp.int32)
        last = jnp.int32(0)
        for number in range(starts_count):
            start = starts_ref[0, number] - (place * spans + span) * SPAN
            inside = (start >= 0) & (start < SPAN)
            at = jnp.where(inside, start, jnp.int32(1 << 20))
            doc_row += (row >= at).astype(jnp.int32)
            doc_col += (col >= at).astype(jnp.int32)
            doc += (row_lanes >= at).astype(jnp.int32)
            last += inside.astype(jnp.int32)
        linked = (doc_row == doc_col) & (col <= row)
        scores = lax.dot_general(
            query.astype(bf16), keys.astype(bf16), (((1,), (1,)), ((), ())),
            preferred_element_type=f32,
        )
        score_ref[span] = jnp.where(linked, scores, 0.0)
        total = cum[SPAN - 1 :, :]
        entry_ref[span] = split_float(jnp.where(doc == 0, jnp.exp(cum), 0.0))
        end_ref[span] = split_float(jnp.where(doc == last, jnp.exp(total - cum), 0.0) * steps)
        cum_ref[span] = cum
        bias = (jnp.log(steps) - cum).T
        for chunk in range(chunks):
            bias_ref[span, chunk] = bias[chunk * heads : (chunk + 1) * heads]
        keys_ref[span] = keys.T.astype(bf16)
        query_ref[span] = query.astype(bf16)
        return total_before + total, restarts + last

    total, restarts = lax.fori_loop(
        0, spans, prepare, (jnp.zeros((1, LANES), f32), jnp.int32(0))
    )
    through = jnp.where(restarts == 0, jnp.exp(total), 0.0)
    through_ref[...] = split_float(jnp.broadcast_to(through, (16, LANES)))
    far_away = list(enumerate(far_distances(shards)))
    reach = range(1, shards - 1) if far_away else ()

    for distance in reach:

        @pl.when((place > 0) & (place + distance < shards))
        def _():
            pltpu.make_async_remote_copy(
                src_ref=through_ref, dst_ref=throughs.at[place],
                send_sem=through_send.at[distance], recv_sem=through_recv.at[place],
                device_id={"seq": jnp.minimum(place + distance, shards - 1)},
                device_id_type=pl.DeviceIdType.MESH,
            ).start()

    for distance in reach:

        @pl.when(place - distance > 0)
        def _():
            source = jnp.maximum(place - distance, 0)
            wait_bytes(throughs.at[source], through_recv.at[source])

    for index, distance in far_away:

        @pl.when(place >= distance)
        def _():
            scale = jnp.ones((16, LANES), f32)
            for back in range(1, distance):
                factor = throughs[jnp.maximum(place - back, 0)].astype(f32)
                scale = scale * (factor[:, :LANES] + factor[:, LANES:])
            far_scale[index] = split_float(scale)

        @pl.when(place < distance)
        def _():
            far_scale[index] = jnp.zeros((16, 2 * LANES), bf16)

    def select_heads(chunk):
        wanted = lax.broadcasted_iota(jnp.int32, (LANES, width), 0) - chunk * heads
        own_head = lax.broadcasted_iota(jnp.int32, (LANES, width), 1) // head_width
        ones = jnp.where(wanted == own_head, 1.0, 0.0).astype(bf16)
        slot = lax.rem(chunk, ring)
        ones_ref[slot, pl.ds(0, LANES), :] = ones
        ones_ref[slot, pl.ds(LANES, LANES), :] = ones

    def span_values(span):
        part = pl.ds(pl.multiple_of(span * RUNS, RUNS), RUNS)
        return values_ref[part].astype(f32).reshape(SPAN, width)

    def far_copy(chunk, hop, index, distance):
        slot = lax.rem(chunk, 2)
        return pltpu.make_async_remote_copy(
            src_ref=leaving.at[slot, hop], dst_ref=far.at[chunk, index],
            send_sem=far_send.at[slot, index], recv_sem=far_recv.at[chunk, index],
            device_id={"seq": jnp.minimum(place + distance, shards - 1)},
            device_id_type=pl.DeviceIdType.MESH,
        )

    def sends_far(hop, distance):
        first = place == 0
        return (place + distance < shards) & (first if hop == 0 else jnp.logical_not(first))

    def pass_on(chunk, hop, state):
        slot = lax.rem(chunk, 2)
        left, send = leaving.at[slot, hop], hop_send.at[slot, hop]

        @pl.when((place < shards - 1) & (chunk > 1))
        def _():
            wait_bytes(left, send)

        for index, distance in far_away:

            @pl.when(sends_far(hop, distance) & (chunk > 1))
            def _():
                wait_bytes(left, far_send.at[slot, index])

        @pl.when(place < shards - 1)
        def _():
            leaving[slot, hop] = state.astype(bf16)
            pltpu.make_async_remote_copy(
                src_ref=left, dst_ref=entering.at[chunk, hop], send_sem=send,
                recv_sem=hop_recv.at[chunk, hop], device_id={"seq": jnp.minimum(place + 1, shards - 1)},
                device_id_type=pl.DeviceIdType.MESH,
            ).start()

        for index, distance in far_away:

            @pl.when(sends_far(hop, distance))
            def _():
                far_copy(chunk, hop, index, distance).start()

    def handed(chunk, hop):
        @pl.when(place > 0)
        def _():
            wait_bytes(entering.at[chunk, hop], hop_recv.at[chunk, hop])

        return jnp.where(place > 0, entering[chunk, hop].astype(f32), 0.0)

    def handed_far(chunk, index, distance, ones):
        @pl.when(place >= distance)
        def _():
            wait_bytes(far.at[chunk, index], far_recv.at[chunk, index])

        scale = spread(far_scale[index], ones)[0:1, :]
        return scale * jnp.where(place >= distance, far[chunk, index].astype(f32), 0.0)

    def take(chunk):
        slot = lax.rem(chunk, ring)
        arrived(landing.at[chunk], own_sem.at[chunk], recv_sem.at[chunk])
        copy = pltpu.make_async_copy(landing.at[chunk], current, current_sem)
        copy.start()

        @pl.when(chunk + AHEAD < chunks)
        def _():
            send_chunk(chunk + AHEAD)

        select_heads(chunk)
        copy.wait()
        final_ref[slot] = jnp.zeros((LANES, width), f32)

        @pl.loop(0, spans)
        def _(span):
            for run in range(RUNS):
                values_ref[span * RUNS + run] = current[pick_ref[0, span * RUNS + run]]
            ones = ones_ref[slot]
            scaled = (span_values(span) * spread(end_ref[span], ones)).astype(bf16)
            added = jnp.dot(keys_ref[span], scaled, preferred_element_type=f32)
            added_ref[slot, span] = added
            kept = spread(entry_ref[span, SPAN - 16 :, :], ones)[15:16, :]
            final_ref[slot] = kept * final_ref[slot] + added

        pass_on(chunk, 0, final_ref[slot])

    def forward(chunk, hop):
        slot = lax.rem(chunk, ring)
        before = handed(chunk, hop - 1)
        kept = spread(through_ref[...], ones_ref[slot])[0:1, :]
        pass_on(chunk, hop, kept * before + final_ref[slot])

    per_tile = LANES // head_width
    lane = lax.broadcasted_iota(jnp.int32, (HALF, LANES), 1) // head_width

    def within(chunk, span):
        values = span_values(span)
        skipped = spread(skip_ref[...], ones_ref[lax.rem(chunk, ring)])[0:1, :] * values
        turn = lax.rem(LANES - chunk * heads, LANES)
        turned_ref[...] = pltpu.roll(cum_ref[span], turn, axis=1)
        bias = bias_ref[span, chunk]
        packed = values.astype(bf16)
        for tile in range(width // LANES):
            inside = slice(tile * LANES, (tile + 1) * LANES)
            for half in range(2):
                rows = slice(half * HALF, (half + 1) * HALF)
                depth = (half + 1) * HALF
                scores = score_ref[span, rows, :depth]
                total = None
                for inner in range(per_tile):
                    head = tile * per_tile + inner
                    gap = turned_ref[rows, head : head + 1] + bias[head : head + 1, :depth]
                    weights = (scores * jnp.exp(jnp.minimum(gap, 60.0))).astype(bf16)
                    piece = jnp.dot(weights, packed[:depth, inside], preferred_element_type=f32)
                    total = piece if total is None else jnp.where(lane == inner, piece, total)
                target = pl.ds(pl.multiple_of(span * SPAN + half * HALF, HALF), HALF)
                column = pl.multiple_of(chunk * width + tile * LANES, LANES)
                out_ref[target, pl.ds(column, LANES)] = (skipped[rows, inside] + total).astype(bf16)

    def complete(chunk):
        slot = lax.rem(chunk, ring)
        arriving = handed(chunk, hops - 1)
        for index, distance in far_away:
            arriving = arriving + handed_far(chunk, index, distance, ones_ref[slot])
        state_ref[...] = arriving
        column = pl.multiple_of(chunk * width, LANES)

        @pl.loop(0, spans)
        def _(span):
            entry = spread(entry_ref[span], ones_ref[slot])
            state = state_ref[...]
            from_state = jnp.dot(query_ref[span], state.astype(bf16), preferred_element_type=f32)
            target = (pl.ds(pl.multiple_of(span * SPAN, SPAN), SPAN), pl.ds(column, width))
            out_ref[target] = (out_ref[target].astype(f32) + from_state * entry).astype(bf16)
            state_ref[...] = entry[SPAN - 1 :, :] * state + added_ref[slot, span]

    @pl.loop(0, chunks + hops)
    def _(step):
        for hop in range(1, hops):

            @pl.when((step >= hop) & (step - hop < chunks))
            def _():
                forward(step - hop, hop)

        @pl.when(step >= hops)
        def _():
            complete(step - hops)

        @pl.when(step < chunks)
        def _():
            take(step)

            @pl.loop(0, spans)
            def _(span):
                within(step, span)

    @pl.loop(chunks - stages, chunks)
    def _(chunk):
        wait_bytes(stage.at[lax.rem(chunk, stages), others], send_sem.at[chunk])

    wait_bytes(small_stage.at[others], send_sem.at[small_at])
    wait_bytes(wanted_runs.at[pl.ds(0, groups - 1)], id_send)

    @pl.when(place < shards - 1)
    def _():
        for slot in range(2):
            for hop in range(hops):
                wait_bytes(leaving.at[slot, hop], hop_send.at[slot, hop])

    for index, distance in far_away:

        @pl.when(place + distance < shards)
        def _():
            for slot in range(2):
                wait_bytes(leaving.at[slot, 0], far_send.at[slot, index])

    for distance in reach:

        @pl.when((place > 0) & (place + distance < shards))
        def _():
            wait_bytes(through_ref, through_send.at[distance])


def flush_kernel(held_ref, out_ref, sems):
    rows = held_ref.shape[0] // sems.shape[0]
    copies = []
    for number in range(sems.shape[0]):
        part = pl.ds(number * rows, rows)
        copies.append(pltpu.make_async_copy(held_ref.at[part], out_ref.at[part], sems.at[number]))
        copies[-1].start()
    for copy in copies:
        copy.wait()


def flush(held):
    return pl.pallas_call(
        flush_kernel,
        in_specs=[pl.BlockSpec(memory_space=pltpu.VMEM)],
        out_specs=ANY,
        out_shape=jax.ShapeDtypeStruct(held.shape, held.dtype),
        scratch_shapes=[pltpu.SemaphoreType.DMA((FLUSHES,))],
        compiler_params=pltpu.CompilerParams(vmem_limit_bytes=1024 * 1024),
        name="flush",
    )(pltpu.with_memory_space_constraint(held, pltpu.VMEM))


def hops_of(shards):
    return min(2, shards - 1)


def far_distances(shards):
    return range(3, shards, 2)


AHEAD = 2
FLUSHES = 10
CHUNK_HEADS = 4
STAGES = 4


def fused(source, starts, tokens, keys, query, steps, decay, gain, groups, shards, capacity):
    runs, _, full = tokens.shape
    heads = decay.shape[1]
    spans = runs // RUNS
    head_width = full // heads
    chunks = heads // CHUNK_HEADS
    width = CHUNK_HEADS * head_width
    hops = hops_of(shards)
    slots = groups * capacity
    smem = pl.BlockSpec(memory_space=pltpu.SMEM)
    vmem = pl.BlockSpec(memory_space=pltpu.VMEM)
    dma = pltpu.SemaphoreType.DMA
    small = 3 * LANES
    ring = hops + 1
    far_count = max(1, len(far_distances(shards)))
    return pl.pallas_call(
        functools.partial(
            fused_kernel, (groups, shards),
            (capacity, spans, chunks, CHUNK_HEADS, head_width, starts.shape[1]),
        ),
        in_specs=[vmem, smem, ANY, ANY, ANY, ANY, vmem, vmem],
        out_specs=vmem,
        out_shape=pltpu.VMEM((runs * SEG, full), bf16),
        scratch_shapes=[
            pltpu.VMEM((1, runs), jnp.int32),
            pltpu.VMEM((groups, 1, runs), jnp.int32),
            pltpu.VMEM((groups, LANES), jnp.int32),
            pltpu.VMEM((1, runs), jnp.int32),
            pltpu.SMEM((groups, LANES), jnp.int32),
            pltpu.SMEM((1, runs), jnp.int32),
            pltpu.VMEM((16, LANES), f32),
            pltpu.VMEM((heads, runs * SEG), bf16),
            pltpu.VMEM((runs, SEG, width), bf16),
            pltpu.VMEM((runs, SEG, small), bf16),
            pltpu.VMEM((STAGES, slots, SEG, width), bf16),
            pltpu.VMEM((slots, SEG, small), bf16),
            pltpu.VMEM((chunks, slots, SEG, width), bf16),
            pltpu.VMEM((slots, SEG, small), bf16),
            pltpu.VMEM((slots, SEG, width), bf16),
            pltpu.VMEM((runs, SEG, width), bf16),
            pltpu.VMEM((ring, spans, LANES, width), f32),
            pltpu.VMEM((ring, LANES, width), f32),
            pltpu.VMEM((spans, SPAN, LANES), f32),
            pltpu.VMEM((spans, chunks, CHUNK_HEADS, SPAN), f32),
            pltpu.VMEM((spans, SPAN, 2 * LANES), bf16),
            pltpu.VMEM((spans, SPAN, 2 * LANES), bf16),
            pltpu.VMEM((spans, LANES, SPAN), bf16),
            pltpu.VMEM((spans, SPAN, LANES), bf16),
            pltpu.VMEM((spans, SPAN, SPAN), f32),
            pltpu.VMEM((16, 2 * LANES), bf16),
            pltpu.VMEM((ring, 2 * LANES, width), bf16),
            pltpu.VMEM((SPAN, LANES), f32),
            pltpu.VMEM((16, 2 * LANES), bf16),
            pltpu.VMEM((LANES, width), f32),
            pltpu.VMEM((2, hops, LANES, width), bf16),
            pltpu.VMEM((chunks, hops, LANES, width), bf16),
            pltpu.VMEM((chunks, far_count, LANES, width), bf16),
            pltpu.VMEM((far_count, 16, 2 * LANES), bf16),
            pltpu.VMEM((shards, 16, 2 * LANES), bf16),
            dma((2,)),
            dma,
            dma,
            dma,
            dma((3,)),
            dma((chunks + 1,)),
            dma((chunks + 1,)),
            dma((chunks + 1,)),
            dma,
            dma((2, hops)),
            dma((chunks, hops)),
            dma((2, far_count)),
            dma((chunks, far_count)),
            dma((shards,)),
            dma((shards,)),
        ],
        compiler_params=params(collective_id=0, has_side_effects=True),
        cost_estimate=pl.CostEstimate(
            flops=8 * runs * SEG * SPAN * full, transcendentals=runs * SEG * SPAN * heads,
            bytes_accessed=4 * runs * SEG * full,
        ),
        name="fused",
    )(source, starts, tokens, keys, query, steps, decay, gain)


def on_device(
    token_rows, key_rows, query_rows, step_rows, decay_log, skip_gain, source_rows, document_starts
):
    tokens, full = token_rows.shape
    groups = lax.axis_size("dp")
    shards = lax.axis_size("seq")
    runs = tokens // SEG
    capacity = runs // groups + 1
    result = fused(
        source_rows, document_starts, token_rows.reshape(runs, SEG, full),
        key_rows.reshape(runs, SEG, LANES), query_rows.reshape(runs, SEG, LANES), step_rows.T,
        decay_log[None, :], skip_gain[None, :], groups, shards, capacity,
    )
    return flush(result)[None]


def solution(mesh):
    in_specs = (
        P(("dp", "seq"), None),
        P(("dp", "seq"), None),
        P(("dp", "seq"), None),
        P(("dp", "seq"), None),
        P(),
        P(),
        P("dp", "seq"),
        P("dp", None),
    )
    out_specs = P("dp", "seq", None)
    return jax.shard_map(
        on_device, mesh=mesh, in_specs=in_specs, out_specs=out_specs, check_vma=False
    )
```

```python
import functools

import jax
import jax.numpy as jnp
from jax import lax
from jax.experimental import pallas as pl
from jax.experimental.pallas import tpu as pltpu
from jax.sharding import PartitionSpec as P

SPAN = 256
SEG = 8
RUNS = SPAN // SEG
HALF = SPAN // 2
LANES = 128

f32, bf16 = jnp.float32, jnp.bfloat16
ANY = pl.BlockSpec(memory_space=pl.ANY)
VMEM_LIMIT = 46 * 1024 * 1024


def params(**more):
    return pltpu.CompilerParams(vmem_limit_bytes=VMEM_LIMIT, **more)


def spread(hilo, ones):
    return jnp.dot(hilo, ones, preferred_element_type=f32)


def split_float(value):
    high = value.astype(bf16)
    low = (value - high.astype(f32)).astype(bf16)
    return jnp.concatenate([high, low], axis=1)


def plan_sends(groups, shards, runs, capacity, me, wanted):
    earlier = lax.broadcasted_iota(jnp.int32, (runs, runs), 0) < lax.broadcasted_iota(
        jnp.int32, (runs, runs), 1
    )
    earlier = jnp.where(earlier, 1.0, 0.0).astype(bf16)

    def ranks(hit):
        ones = jnp.where(hit, 1.0, 0.0).astype(bf16)
        return jnp.dot(ones, earlier, preferred_element_type=f32).astype(jnp.int32)

    mine = (wanted // runs) // shards == me
    local = wanted % runs
    rank = ranks(mine)
    lane = lax.broadcasted_iota(jnp.int32, (groups, LANES), 1)
    send = jnp.zeros((groups, LANES), jnp.int32)
    for slot in range(capacity):
        chosen = jnp.sum(jnp.where(mine & (rank == slot), local, 0), axis=1, keepdims=True)
        send = jnp.where(lane == slot, chosen, send)
    return send, ranks


def plan_picks(groups, shards, runs, capacity, own, ranks):
    source = (own // runs) // shards
    group = lax.broadcasted_iota(jnp.int32, (groups, runs), 0)
    hit = jnp.broadcast_to(source, (groups, runs)) == group
    return jnp.sum(jnp.where(hit, group * capacity + ranks(hit), 0), axis=0, keepdims=True)


def fused_kernel(
    axes, sizes, source_ref, starts_ref, tokens_hbm, key_hbm, query_hbm, step_hbm, decay_log_ref, gain_ref, out_ref,
    own_runs, wanted_runs, plan_ref, choice_ref, send_ref, pick_ref, head_ref, turned_steps,
    token, small, stage, small_stage, landing, small_landing, current, values_ref, added_ref, final_ref,
    cum_ref, bias_ref, entry_ref, end_ref, keys_ref, query_ref, score_ref, through_ref,
    ones_ref, turned_ref, skip_ref, state_ref, leaving, entering, far, far_scale, throughs,
    plan_sem, id_send, id_recv,
    token_sem, small_sem, own_sem, send_sem, recv_sem, current_sem, hop_send, hop_recv, far_send, far_recv, through_send, through_recv,
):
    groups, shards = axes
    capacity, spans, chunks, heads, head_width, starts_count = sizes
    ring = hops_of(shards) + 1
    small_at = chunks
    width = heads * head_width
    hops = hops_of(shards)
    runs = spans * RUNS
    all_heads = chunks * heads
    me = lax.axis_index("dp")
    place = lax.axis_index("seq")

    def token_copy(chunk):
        column = pl.multiple_of(chunk * width, LANES)
        return pltpu.make_async_copy(
            tokens_hbm.at[:, :, pl.ds(column, width)], token, token_sem
        )

    small_parts = [
        pltpu.make_async_copy(key_hbm, small.at[:, :, pl.ds(0, LANES)], small_sem.at[0]),
        pltpu.make_async_copy(query_hbm, small.at[:, :, pl.ds(LANES, LANES)], small_sem.at[1]),
        pltpu.make_async_copy(step_hbm, turned_steps, small_sem.at[2]),
    ]
    token_copy(0).start()
    for part in small_parts:
        part.start()

    barrier = pltpu.get_barrier_semaphore()

    def greet(**device):
        pl.semaphore_signal(barrier, inc=1, device_id=device, device_id_type=pl.DeviceIdType.MESH)

    @pl.loop(1, groups)
    def _(distance):
        greet(dp=lax.rem(me + distance, groups))

    @pl.loop(1, shards)
    def _(distance):
        greet(seq=lax.rem(place + distance, shards))

    every = lax.broadcasted_iota(jnp.int32, (runs * SEG, runs), 0) == SEG * lax.broadcasted_iota(
        jnp.int32, (runs * SEG, runs), 1
    )
    every = jnp.where(every, 1.0, 0.0).astype(bf16)
    numbers = source_ref[...] // SEG
    parts = [((numbers >> shift) & 255).astype(f32).astype(bf16) for shift in (0, 8, 16)]
    own = jnp.dot(
        jnp.concatenate([jnp.broadcast_to(part, (8, runs * SEG)) for part in parts], axis=0), every,
        preferred_element_type=f32,
    ).astype(jnp.int32)
    own = own[0:1] + own[8:9] * 256 + own[16:17] * 65536
    own_runs[...] = own
    wanted_runs[me] = own
    pl.semaphore_wait(barrier, groups - 1 + shards - 1)

    @pl.loop(1, groups)
    def _(distance):
        group = lax.rem(me + distance, groups)
        pltpu.make_async_remote_copy(
            src_ref=own_runs, dst_ref=wanted_runs.at[me], send_sem=id_send, recv_sem=id_recv,
            device_id={"dp": group}, device_id_type=pl.DeviceIdType.MESH,
        ).start()

    def wait_bytes(ref, sem):
        pltpu.make_async_copy(ref, ref, sem).wait()

    wait_bytes(wanted_runs.at[pl.ds(0, groups - 1)], id_recv)
    wanted = jnp.concatenate([wanted_runs[group] for group in range(groups)], axis=0)
    plan_ref[...], ranks = plan_sends(groups, shards, runs, capacity, me, wanted)
    plan_copy = pltpu.make_async_copy(plan_ref, send_ref, plan_sem.at[0])
    plan_copy.start()
    choice_ref[...] = plan_picks(groups, shards, runs, capacity, own, ranks)
    choice_copy = pltpu.make_async_copy(choice_ref, pick_ref, plan_sem.at[1])
    choice_copy.start()
    plan_copy.wait()

    def scatter(source, buffer, target, sems):
        own_done, send, recv = sems

        def gather(group):
            start = group * capacity
            for slot in range(capacity):
                buffer[start + slot] = source[send_ref[group, slot]]
            return pl.ds(start, capacity)

        home = pl.ds(me * capacity, capacity)

        @pl.loop(1, groups)
        def _(distance):
            group = lax.rem(me + distance, groups)
            part = gather(group)
            pltpu.make_async_remote_copy(
                src_ref=buffer.at[part], dst_ref=target.at[home],
                send_sem=send, recv_sem=recv, device_id={"dp": group},
                device_id_type=pl.DeviceIdType.MESH,
            ).start()

        part = gather(me)
        pltpu.make_async_copy(
            buffer.at[part], target.at[home], own_done
        ).start()

    others = pl.ds(0, (groups - 1) * capacity)
    single = pl.ds(0, capacity)

    def arrived(target, own, recv):
        wait_bytes(target.at[others], recv)
        wait_bytes(target.at[single], own)

    stages = stage.shape[0]

    def send_chunk(chunk):
        slot = lax.rem(chunk, stages)
        token_copy(chunk).wait()

        @pl.when(chunk >= stages)
        def _():
            wait_bytes(stage.at[slot, others], send_sem.at[chunk - stages])

        scatter(
            token, stage.at[slot], landing.at[chunk],
            (own_sem.at[chunk], send_sem.at[chunk], recv_sem.at[chunk]),
        )

        @pl.when(chunk + 1 < chunks)
        def _():
            token_copy(chunk + 1).start()

    send_chunk(jnp.int32(0))
    for part in small_parts:
        part.wait()
    steps_across = turned_steps[...].astype(f32)
    steps_across = jnp.concatenate(
        [steps_across, jnp.zeros((LANES - all_heads, runs * SEG), f32)], axis=0
    )
    small[:, :, 2 * LANES :] = steps_across.T.reshape(runs, SEG, LANES).astype(bf16)
    scatter(
        small, small_stage, small_landing,
        (own_sem.at[small_at], send_sem.at[small_at], recv_sem.at[small_at]),
    )
    choice_copy.wait()
    @pl.loop(1, AHEAD)
    def _(chunk):
        send_chunk(chunk)

    head_ref[...] = jnp.zeros_like(head_ref)
    head_ref[0:1, :all_heads] = decay_log_ref[...]
    head_ref[8:9, :all_heads] = gain_ref[...]
    skip_ref[...] = split_float(jnp.broadcast_to(head_ref[8:9, :], (16, LANES)))
    arrived(small_landing, own_sem.at[small_at], recv_sem.at[small_at])

    row = lax.broadcasted_iota(jnp.int32, (SPAN, SPAN), 0)
    col = lax.broadcasted_iota(jnp.int32, (SPAN, SPAN), 1)
    row_lanes = lax.broadcasted_iota(jnp.int32, (SPAN, LANES), 0)

    def prepare(span, carry):
        total_before, restarts = carry
        picked = jnp.stack(
            [small_landing[pick_ref[0, span * RUNS + run]].astype(f32) for run in range(RUNS)]
        ).reshape(SPAN, 3 * LANES)
        keys = picked[:, :LANES]
        query = picked[:, LANES : 2 * LANES]
        raw = picked[:, 2 * LANES :]
        steps = jnp.maximum(raw, 0.0) + jnp.log1p(jnp.exp(-jnp.abs(raw)))
        log_decay = -steps * jnp.exp(head_ref[0:1, :])
        lower = jnp.where(col <= row, 1.0, 0.0)
        cum = jnp.dot(lower, log_decay, precision=lax.Precision.HIGHEST, preferred_element_type=f32)
        doc_row = jnp.zeros((SPAN, SPAN), jnp.int32)
        doc_col = jnp.zeros((SPAN, SPAN), jnp.int32)
        doc = jnp.zeros((SPAN, LANES), jnp.int32)
        last = jnp.int32(0)
        for number in range(starts_count):
            start = starts_ref[0, number] - (place * spans + span) * SPAN
            inside = (start >= 0) & (start < SPAN)
            at = jnp.where(inside, start, jnp.int32(1 << 20))
            doc_row += (row >= at).astype(jnp.int32)
            doc_col += (col >= at).astype(jnp.int32)
            doc += (row_lanes >= at).astype(jnp.int32)
            last += inside.astype(jnp.int32)
        linked = (doc_row == doc_col) & (col <= row)
        scores = lax.dot_general(
            query.astype(bf16), keys.astype(bf16), (((1,), (1,)), ((), ())),
            preferred_element_type=f32,
        )
        score_ref[span] = jnp.where(linked, scores, 0.0)
        total = cum[SPAN - 1 :, :]
        entry_ref[span] = split_float(jnp.where(doc == 0, jnp.exp(cum), 0.0))
        end_ref[span] = split_float(jnp.where(doc == last, jnp.exp(total - cum), 0.0) * steps)
        cum_ref[span] = cum
        bias = (jnp.log(steps) - cum).T
        for chunk in range(chunks):
            bias_ref[span, chunk] = bias[chunk * heads : (chunk + 1) * heads]
        keys_ref[span] = keys.T.astype(bf16)
        query_ref[span] = query.astype(bf16)
        return total_before + total, restarts + last

    total, restarts = lax.fori_loop(
        0, spans, prepare, (jnp.zeros((1, LANES), f32), jnp.int32(0))
    )
    through = jnp.where(restarts == 0, jnp.exp(total), 0.0)
    through_ref[...] = split_float(jnp.broadcast_to(through, (16, LANES)))
    far_away = list(enumerate(far_distances(shards)))
    reach = range(1, shards - 1) if far_away else ()

    for distance in reach:

        @pl.when((place > 0) & (place + distance < shards))
        def _():
            pltpu.make_async_remote_copy(
                src_ref=through_ref, dst_ref=throughs.at[place],
                send_sem=through_send.at[distance], recv_sem=through_recv.at[place],
                device_id={"seq": jnp.minimum(place + distance, shards - 1)},
                device_id_type=pl.DeviceIdType.MESH,
            ).start()

    for distance in reach:

        @pl.when(place - distance > 0)
        def _():
            source = jnp.maximum(place - distance, 0)
            wait_bytes(throughs.at[source], through_recv.at[source])

    for index, distance in far_away:

        @pl.when(place >= distance)
        def _():
            scale = jnp.ones((16, LANES), f32)
            for back in range(1, distance):
                factor = throughs[jnp.maximum(place - back, 0)].astype(f32)
                scale = scale * (factor[:, :LANES] + factor[:, LANES:])
            far_scale[index] = split_float(scale)

        @pl.when(place < distance)
        def _():
            far_scale[index] = jnp.zeros((16, 2 * LANES), bf16)

    def select_heads(chunk):
        wanted = lax.broadcasted_iota(jnp.int32, (LANES, width), 0) - chunk * heads
        own_head = lax.broadcasted_iota(jnp.int32, (LANES, width), 1) // head_width
        ones = jnp.where(wanted == own_head, 1.0, 0.0).astype(bf16)
        slot = lax.rem(chunk, ring)
        ones_ref[slot, pl.ds(0, LANES), :] = ones
        ones_ref[slot, pl.ds(LANES, LANES), :] = ones

    def span_values(span):
        part = pl.ds(pl.multiple_of(span * RUNS, RUNS), RUNS)
        return values_ref[part].astype(f32).reshape(SPAN, width)

    def far_copy(chunk, hop, index, distance):
        slot = lax.rem(chunk, 2)
        return pltpu.make_async_remote_copy(
            src_ref=leaving.at[slot, hop], dst_ref=far.at[chunk, index],
            send_sem=far_send.at[slot, index], recv_sem=far_recv.at[chunk, index],
            device_id={"seq": jnp.minimum(place + distance, shards - 1)},
            device_id_type=pl.DeviceIdType.MESH,
        )

    def sends_far(hop, distance):
        first = place == 0
        return (place + distance < shards) & (first if hop == 0 else jnp.logical_not(first))

    def pass_on(chunk, hop, state):
        slot = lax.rem(chunk, 2)
        left, send = leaving.at[slot, hop], hop_send.at[slot, hop]

        @pl.when((place < shards - 1) & (chunk > 1))
        def _():
            wait_bytes(left, send)

        for index, distance in far_away:

            @pl.when(sends_far(hop, distance) & (chunk > 1))
            def _():
                wait_bytes(left, far_send.at[slot, index])

        @pl.when(place < shards - 1)
        def _():
            leaving[slot, hop] = state.astype(bf16)
            pltpu.make_async_remote_copy(
                src_ref=left, dst_ref=entering.at[chunk, hop], send_sem=send,
                recv_sem=hop_recv.at[chunk, hop], device_id={"seq": jnp.minimum(place + 1, shards - 1)},
                device_id_type=pl.DeviceIdType.MESH,
            ).start()

        for index, distance in far_away:

            @pl.when(sends_far(hop, distance))
            def _():
                far_copy(chunk, hop, index, distance).start()

    def handed(chunk, hop):
        @pl.when(place > 0)
        def _():
            wait_bytes(entering.at[chunk, hop], hop_recv.at[chunk, hop])

        return jnp.where(place > 0, entering[chunk, hop].astype(f32), 0.0)

    def handed_far(chunk, index, distance, ones):
        @pl.when(place >= distance)
        def _():
            wait_bytes(far.at[chunk, index], far_recv.at[chunk, index])

        scale = spread(far_scale[index], ones)[0:1, :]
        return scale * jnp.where(place >= distance, far[chunk, index].astype(f32), 0.0)

    def take(chunk):
        slot = lax.rem(chunk, ring)
        arrived(landing.at[chunk], own_sem.at[chunk], recv_sem.at[chunk])
        copy = pltpu.make_async_copy(landing.at[chunk], current, current_sem)
        copy.start()

        @pl.when(chunk + AHEAD < chunks)
        def _():
            send_chunk(chunk + AHEAD)

        select_heads(chunk)
        copy.wait()
        final_ref[slot] = jnp.zeros((LANES, width), f32)

        @pl.loop(0, spans, unroll=True)
        def _(span):
            for run in range(RUNS):
                values_ref[span * RUNS + run] = current[pick_ref[0, span * RUNS + run]]
            ones = ones_ref[slot]
            scaled = (span_values(span) * spread(end_ref[span], ones)).astype(bf16)
            added = jnp.dot(keys_ref[span], scaled, preferred_element_type=f32)
            added_ref[slot, span] = added
            kept = spread(entry_ref[span, SPAN - 16 :, :], ones)[15:16, :]
            final_ref[slot] = kept * final_ref[slot] + added

        pass_on(chunk, 0, final_ref[slot])

    def forward(chunk, hop):
        slot = lax.rem(chunk, ring)
        before = handed(chunk, hop - 1)
        kept = spread(through_ref[...], ones_ref[slot])[0:1, :]
        pass_on(chunk, hop, kept * before + final_ref[slot])

    per_tile = LANES // head_width
    lane = lax.broadcasted_iota(jnp.int32, (HALF, LANES), 1) // head_width

    def within(chunk, span):
        values = span_values(span)
        skipped = spread(skip_ref[...], ones_ref[lax.rem(chunk, ring)])[0:1, :] * values
        turn = lax.rem(LANES - chunk * heads, LANES)
        turned_ref[...] = pltpu.roll(cum_ref[span], turn, axis=1)
        bias = bias_ref[span, chunk]
        packed = values.astype(bf16)
        for tile in range(width // LANES):
            inside = slice(tile * LANES, (tile + 1) * LANES)
            for half in range(2):
                rows = slice(half * HALF, (half + 1) * HALF)
                depth = (half + 1) * HALF
                scores = score_ref[span, rows, :depth]
                total = None
                for inner in range(per_tile):
                    head = tile * per_tile + inner
                    gap = turned_ref[rows, head : head + 1] + bias[head : head + 1, :depth]
                    weights = (scores * jnp.exp(jnp.minimum(gap, 60.0))).astype(bf16)
                    piece = jnp.dot(weights, packed[:depth, inside], preferred_element_type=f32)
                    total = piece if total is None else jnp.where(lane == inner, piece, total)
                target = pl.ds(pl.multiple_of(span * SPAN + half * HALF, HALF), HALF)
                column = pl.multiple_of(chunk * width + tile * LANES, LANES)
                out_ref[target, pl.ds(column, LANES)] = (skipped[rows, inside] + total).astype(bf16)

    def complete(chunk):
        slot = lax.rem(chunk, ring)
        arriving = handed(chunk, hops - 1)
        for index, distance in far_away:
            arriving = arriving + handed_far(chunk, index, distance, ones_ref[slot])
        state_ref[...] = arriving
        column = pl.multiple_of(chunk * width, LANES)

        @pl.loop(0, spans, unroll=True)
        def _(span):
            entry = spread(entry_ref[span], ones_ref[slot])
            state = state_ref[...]
            from_state = jnp.dot(query_ref[span], state.astype(bf16), preferred_element_type=f32)
            target = (pl.ds(pl.multiple_of(span * SPAN, SPAN), SPAN), pl.ds(column, width))
            out_ref[target] = (out_ref[target].astype(f32) + from_state * entry).astype(bf16)
            state_ref[...] = entry[SPAN - 1 :, :] * state + added_ref[slot, span]

    @pl.loop(0, chunks + hops)
    def _(step):
        for hop in range(1, hops):

            @pl.when((step >= hop) & (step - hop < chunks))
            def _():
                forward(step - hop, hop)

        @pl.when(step >= hops)
        def _():
            complete(step - hops)

        @pl.when(step < chunks)
        def _():
            take(step)

            @pl.loop(0, spans)
            def _(span):
                within(step, span)

    @pl.loop(chunks - stages, chunks)
    def _(chunk):
        wait_bytes(stage.at[lax.rem(chunk, stages), others], send_sem.at[chunk])

    wait_bytes(small_stage.at[others], send_sem.at[small_at])
    wait_bytes(wanted_runs.at[pl.ds(0, groups - 1)], id_send)

    @pl.when(place < shards - 1)
    def _():
        for slot in range(2):
            for hop in range(hops):
                wait_bytes(leaving.at[slot, hop], hop_send.at[slot, hop])

    for index, distance in far_away:

        @pl.when(place + distance < shards)
        def _():
            for slot in range(2):
                wait_bytes(leaving.at[slot, 0], far_send.at[slot, index])

    for distance in reach:

        @pl.when((place > 0) & (place + distance < shards))
        def _():
            wait_bytes(through_ref, through_send.at[distance])


def flush_kernel(held_ref, out_ref, sems):
    rows = held_ref.shape[0] // sems.shape[0]
    copies = []
    for number in range(sems.shape[0]):
        part = pl.ds(number * rows, rows)
        copies.append(pltpu.make_async_copy(held_ref.at[part], out_ref.at[part], sems.at[number]))
        copies[-1].start()
    for copy in copies:
        copy.wait()


def flush(held):
    return pl.pallas_call(
        flush_kernel,
        in_specs=[pl.BlockSpec(memory_space=pltpu.VMEM)],
        out_specs=ANY,
        out_shape=jax.ShapeDtypeStruct(held.shape, held.dtype),
        scratch_shapes=[pltpu.SemaphoreType.DMA((FLUSHES,))],
        compiler_params=pltpu.CompilerParams(vmem_limit_bytes=1024 * 1024),
        name="flush",
    )(pltpu.with_memory_space_constraint(held, pltpu.VMEM))


def hops_of(shards):
    return min(2, shards - 1)


def far_distances(shards):
    return range(3, shards, 2)


AHEAD = 2
FLUSHES = 10
CHUNK_HEADS = 4
STAGES = 4


def fused(source, starts, tokens, keys, query, steps, decay, gain, groups, shards, capacity):
    runs, _, full = tokens.shape
    heads = decay.shape[1]
    spans = runs // RUNS
    head_width = full // heads
    chunks = heads // CHUNK_HEADS
    width = CHUNK_HEADS * head_width
    hops = hops_of(shards)
    slots = groups * capacity
    smem = pl.BlockSpec(memory_space=pltpu.SMEM)
    vmem = pl.BlockSpec(memory_space=pltpu.VMEM)
    dma = pltpu.SemaphoreType.DMA
    small = 3 * LANES
    ring = hops + 1
    far_count = max(1, len(far_distances(shards)))
    return pl.pallas_call(
        functools.partial(
            fused_kernel, (groups, shards),
            (capacity, spans, chunks, CHUNK_HEADS, head_width, starts.shape[1]),
        ),
        in_specs=[vmem, smem, ANY, ANY, ANY, ANY, vmem, vmem],
        out_specs=vmem,
        out_shape=pltpu.VMEM((runs * SEG, full), bf16),
        scratch_shapes=[
            pltpu.VMEM((1, runs), jnp.int32),
            pltpu.VMEM((groups, 1, runs), jnp.int32),
            pltpu.VMEM((groups, LANES), jnp.int32),
            pltpu.VMEM((1, runs), jnp.int32),
            pltpu.SMEM((groups, LANES), jnp.int32),
            pltpu.SMEM((1, runs), jnp.int32),
            pltpu.VMEM((16, LANES), f32),
            pltpu.VMEM((heads, runs * SEG), bf16),
            pltpu.VMEM((runs, SEG, width), bf16),
            pltpu.VMEM((runs, SEG, small), bf16),
            pltpu.VMEM((STAGES, slots, SEG, width), bf16),
            pltpu.VMEM((slots, SEG, small), bf16),
            pltpu.VMEM((chunks, slots, SEG, width), bf16),
            pltpu.VMEM((slots, SEG, small), bf16),
            pltpu.VMEM((slots, SEG, width), bf16),
            pltpu.VMEM((runs, SEG, width), bf16),
            pltpu.VMEM((ring, spans, LANES, width), f32),
            pltpu.VMEM((ring, LANES, width), f32),
            pltpu.VMEM((spans, SPAN, LANES), f32),
            pltpu.VMEM((spans, chunks, CHUNK_HEADS, SPAN), f32),
            pltpu.VMEM((spans, SPAN, 2 * LANES), bf16),
            pltpu.VMEM((spans, SPAN, 2 * LANES), bf16),
            pltpu.VMEM((spans, LANES, SPAN), bf16),
            pltpu.VMEM((spans, SPAN, LANES), bf16),
            pltpu.VMEM((spans, SPAN, SPAN), f32),
            pltpu.VMEM((16, 2 * LANES), bf16),
            pltpu.VMEM((ring, 2 * LANES, width), bf16),
            pltpu.VMEM((SPAN, LANES), f32),
            pltpu.VMEM((16, 2 * LANES), bf16),
            pltpu.VMEM((LANES, width), f32),
            pltpu.VMEM((2, hops, LANES, width), bf16),
            pltpu.VMEM((chunks, hops, LANES, width), bf16),
            pltpu.VMEM((chunks, far_count, LANES, width), bf16),
            pltpu.VMEM((far_count, 16, 2 * LANES), bf16),
            pltpu.VMEM((shards, 16, 2 * LANES), bf16),
            dma((2,)),
            dma,
            dma,
            dma,
            dma((3,)),
            dma((chunks + 1,)),
            dma((chunks + 1,)),
            dma((chunks + 1,)),
            dma,
            dma((2, hops)),
            dma((chunks, hops)),
            dma((2, far_count)),
            dma((chunks, far_count)),
            dma((shards,)),
            dma((shards,)),
        ],
        compiler_params=params(collective_id=0, has_side_effects=True),
        cost_estimate=pl.CostEstimate(
            flops=8 * runs * SEG * SPAN * full, transcendentals=runs * SEG * SPAN * heads,
            bytes_accessed=4 * runs * SEG * full,
        ),
        name="fused",
    )(source, starts, tokens, keys, query, steps, decay, gain)


def on_device(
    token_rows, key_rows, query_rows, step_rows, decay_log, skip_gain, source_rows, document_starts
):
    tokens, full = token_rows.shape
    groups = lax.axis_size("dp")
    shards = lax.axis_size("seq")
    runs = tokens // SEG
    capacity = runs // groups + 1
    result = fused(
        source_rows, document_starts, token_rows.reshape(runs, SEG, full),
        key_rows.reshape(runs, SEG, LANES), query_rows.reshape(runs, SEG, LANES), step_rows.T,
        decay_log[None, :], skip_gain[None, :], groups, shards, capacity,
    )
    return flush(result)[None]


def solution(mesh):
    in_specs = (
        P(("dp", "seq"), None),
        P(("dp", "seq"), None),
        P(("dp", "seq"), None),
        P(("dp", "seq"), None),
        P(),
        P(),
        P("dp", "seq"),
        P("dp", None),
    )
    out_specs = P("dp", "seq", None)
    return jax.shard_map(
        on_device, mesh=mesh, in_specs=in_specs, out_specs=out_specs, check_vma=False
    )
```
